32 devices in a mesh: ctx: 4 (over z), section: 2 (over x), mp: 4 (over y, core).
Axes of the slice: x: 2, y: 2, z: 4, core: 2. Of those that a mesh axis runs over, the one named last changes fastest.
Arguments:
- patches: bfloat16 [2, 768, 3200], P(None, ('ctx', 'mp')), may hold values from -16 to 16
- carried: bfloat16 [768, 3200], P(('ctx', 'mp')), may hold values from -16 to 16
- norm_gain: float32 [2, 3200], P('section'), may hold values from 0.1 to 1.9
- q_gain: float32 [2, 128], P('section'), may hold values from 1.5 to 2.5
- k_gain: float32 [2, 128], P('section'), may hold values from 1.5 to 2.5
- q_weight: bfloat16 [2, 3200, 2048], P('section', None, 'mp'), may hold values from -0.109375 to 0.109375
- k_weight: bfloat16 [2, 3200, 2048], P('section', None, 'mp'), may hold values from -0.109375 to 0.109375
- v_weight: bfloat16 [2, 3200, 2048], P('section', None, 'mp'), may hold values from -0.109375 to 0.109375
- o_weight: bfloat16 [2, 2048, 3200], P('section', 'mp', 'ctx'), may hold values from -0.125 to 0.125
Outputs:
- section_outputs: bfloat16 [2, 2, 768, 3200], P('section', None, ('ctx', 'mp'))
The draws below stay inside these ranges and needn't reach their ends.
All inputs are finite; a program needn't handle non-finite values.
Results may differ from the reference program's by a relative error of at most 0.0063.
Values may be sent and summed in bfloat16 or wider, within the bound.
A program may use at most 128 MiB of HBM per device.

```python
import math
import jax
import jax.numpy as jnp
from jax import lax

D = 3200
HD = 128
HEADS = 16
MICRO = 2
LAYERS = 2
SEQ = 768


def scaled_rows(key, shape):
    first, second, third = jax.random.split(key, 3)
    row_scale = jnp.exp(jax.random.uniform(first, shape[:-1] + (1,), jnp.float32, -1.15, 1.15))
    column_scale = jnp.exp(jax.random.uniform(second, (shape[-1],), jnp.float32, -1.15, 1.15))
    base = jax.random.normal(third, shape, jnp.float32)
    return jnp.clip(base * row_scale * column_scale, -16.0, 16.0)


def draw_patches(key, part):
    return scaled_rows(jax.random.fold_in(key, 11), (MICRO, SEQ, D)).astype(jnp.bfloat16)


def draw_carried(key, part):
    return scaled_rows(jax.random.fold_in(key, 23), (SEQ, D)).astype(jnp.bfloat16)


def block_scale(own_key, dims, cuts, smallest, high):
    loudness = 1.0
    for dim, shards_of in cuts:
        steps = jax.random.uniform(jax.random.fold_in(jax.random.fold_in(own_key, 6), dim), (shards_of,), jnp.float32, smallest / len(cuts), high / len(cuts))
        loudness = loudness * jnp.repeat(jnp.exp(steps), dims[dim] // shards_of).reshape((-1,) + (1,) * (len(dims) - 1 - dim))
    return loudness


def normal_values(own_key, dims, scale, bound, pieces=(), held_as=jnp.bfloat16):
    drawn = jax.random.normal(own_key, dims, jnp.float32) * scale
    if len(pieces) > 0:
        drawn = block_scale(own_key, dims, pieces, -0.22, 0.18) * drawn
    return jnp.clip(drawn, min=-bound, max=bound).astype(held_as)


def setup_inputs(seed: int = 0) -> dict:
    keys = jax.random.split(jax.random.key(seed), 10)
    patches = draw_patches(jax.random.fold_in(keys[9], 71), 0)
    carried = draw_carried(jax.random.fold_in(keys[9], 71), 0)
    norm_gain = jnp.clip(1.0 + 0.18 * jax.random.normal(keys[2], (LAYERS, D), jnp.float32), 0.1, 1.9)
    q_gain = jnp.clip(1.5 + 1.0 * jax.random.uniform(keys[3], (LAYERS, HD), jnp.float32) ** block_scale(keys[3], (LAYERS, HD), ((0, 2),), -0.2, 0.2), 1.5, 2.5)
    k_gain = jnp.clip(1.5 + 1.0 * jax.random.uniform(keys[4], (LAYERS, HD), jnp.float32) ** block_scale(keys[4], (LAYERS, HD), ((0, 2),), -0.2, 0.2), 1.5, 2.5)
    q_weight = normal_values(keys[5], (LAYERS, D, HEADS * HD), D ** -0.5, 0.109375, ((0, 2), (2, 4)))
    k_weight = normal_values(keys[6], (LAYERS, D, HEADS * HD), D ** -0.5, 0.109375, ((0, 2), (2, 4)))
    v_weight = normal_values(keys[7], (LAYERS, D, HEADS * HD), D ** -0.5, 0.109375, ((0, 2), (2, 4)))
    o_weight = normal_values(keys[8], (LAYERS, HEADS * HD, D), (HEADS * HD) ** -0.5, 0.125, ((0, 2), (1, 4), (2, 4)))
    return dict(patches=patches, carried=carried, norm_gain=norm_gain, q_gain=q_gain, k_gain=k_gain, q_weight=q_weight, k_weight=k_weight, v_weight=v_weight, o_weight=o_weight)


epsilon = 1e-06

def rms_scaled(values, gain):
    return values * lax.rsqrt(lax.optimization_barrier(jnp.mean(values * values, axis=-1, keepdims=True)) + epsilon) * gain

def encoder_layer(row_block, layer_gain, query_gain, key_gain, query_weight, key_weight, value_weight, out_weight):
    count = row_block.shape[0]
    head_dim = query_gain.shape[0]
    head_count = query_weight.shape[1] // head_dim
    score_scale = 1.0 / math.sqrt(head_dim)
    normed = rms_scaled(row_block.astype(jnp.float32), layer_gain).astype(jnp.bfloat16)
    raw_query = jnp.dot(normed, query_weight, preferred_element_type=jnp.float32).reshape(count, head_count, head_dim)
    raw_key = jnp.dot(normed, key_weight, preferred_element_type=jnp.float32).reshape(count, head_count, head_dim)
    raw_value = jnp.dot(normed, value_weight, preferred_element_type=jnp.float32).reshape(count, head_count, head_dim)
    queries = rms_scaled(raw_query, query_gain).astype(jnp.bfloat16)
    key_rows = rms_scaled(raw_key, key_gain).astype(jnp.bfloat16)
    value_rows = raw_value.astype(jnp.bfloat16)

    def one_head(operands):
        head_query, head_key, head_value = operands
        scores = jnp.dot(head_query, head_key.T, preferred_element_type=jnp.float32) * score_scale
        probs = jnp.exp(scores)
        totals = lax.optimization_barrier(jnp.sum(probs, axis=1, keepdims=True))
        weighted = jnp.dot(probs.astype(jnp.bfloat16), head_value, preferred_element_type=jnp.float32)
        return weighted / totals
    stacked = lax.map(one_head, (jnp.transpose(queries, (1, 0, 2)), jnp.transpose(key_rows, (1, 0, 2)), jnp.transpose(value_rows, (1, 0, 2))))
    attended = jnp.transpose(stacked, (1, 0, 2)).reshape(count, head_count * head_dim).astype(jnp.bfloat16)
    summed = row_block.astype(jnp.float32) + jnp.dot(attended, out_weight, preferred_element_type=jnp.float32)
    return summed.astype(jnp.bfloat16)

def reference(patches, carried, norm_gain, q_gain, k_gain, q_weight, k_weight, v_weight, o_weight):

    def run_layer(layer, row_block):
        return encoder_layer(row_block, norm_gain[layer], q_gain[layer], k_gain[layer], q_weight[layer], k_weight[layer], v_weight[layer], o_weight[layer])
    first_layer = [run_layer(0, patches[moment]) for moment in range(MICRO)]
    second_layer = [run_layer(1, carried)]
    for moment in range(1, MICRO):
        second_layer.append(run_layer(1, first_layer[moment - 1]))
    return jnp.stack([jnp.stack(first_layer), jnp.stack(second_layer)])
```

```python
import functools
import math

import jax
import jax.numpy as jnp
from jax import lax
from jax.experimental import pallas as pl
from jax.experimental.pallas import tpu as pltpu
from jax.sharding import PartitionSpec as P

epsilon = 1e-06


def rms_scaled(values, gain):
    return values * lax.rsqrt(jnp.mean(values * values, axis=-1, keepdims=True) + epsilon) * gain


def shifted(value, axis, steps):
    count = lax.axis_size(axis)
    leading, last = (max(0, -steps), min(count, count - steps))
    return lax.ppermute(value, axis, [(source, source + steps) for source in range(leading, last)])


def per_device(patches, carried, norm_gain, q_gain, k_gain, q_weight, k_weight, v_weight, o_weight):
    micro_count = patches.shape[0]
    head_dim = q_gain.shape[1]
    head_count = q_weight.shape[2] // head_dim
    columns = head_count * head_dim
    score_scale = 1.0 / math.sqrt(head_dim)
    section_index = lax.axis_index("section")
    incoming = carried
    results = []
    out_weight = lax.all_gather(o_weight[0], "ctx", axis=1, tiled=True)
    for micro_step in range(micro_count):
        layer_input = jnp.where(section_index == 0, patches[micro_step], incoming)
        residual = layer_input.astype(jnp.float32)
        normed = rms_scaled(residual, norm_gain[0]).astype(jnp.bfloat16)
        segment = lax.all_gather(normed, "mp", axis=0, tiled=True)
        rows = segment.shape[0]
        raw_query = jnp.dot(segment, q_weight[0], preferred_element_type=jnp.float32)
        raw_key = jnp.dot(segment, k_weight[0], preferred_element_type=jnp.float32)
        raw_value = jnp.dot(segment, v_weight[0], preferred_element_type=jnp.float32)
        queries = rms_scaled(raw_query.reshape(rows, head_count, head_dim), q_gain[0])
        keys = rms_scaled(raw_key.reshape(rows, head_count, head_dim), k_gain[0])
        keys = keys.astype(jnp.bfloat16).reshape(rows, columns)
        key_block = lax.all_gather(keys, "ctx", axis=0, tiled=True)
        value_block = lax.all_gather(raw_value.astype(jnp.bfloat16), "ctx", axis=0, tiled=True)
        count = key_block.shape[0]
        scores = score_scale * jnp.einsum(
            "qhd,khd->qhk",
            queries.astype(jnp.bfloat16),
            key_block.reshape(count, head_count, head_dim),
            preferred_element_type=jnp.float32,
        )
        probs = jnp.exp(scores)
        totals = jnp.sum(probs, axis=2)
        weighted = jnp.einsum(
            "qhk,khd->qhd",
            probs.astype(jnp.bfloat16),
            value_block.reshape(count, head_count, head_dim),
            preferred_element_type=jnp.float32,
        )
        attended = (weighted / totals[:, :, None]).reshape(rows, columns).astype(jnp.bfloat16)
        partial_value = jnp.dot(attended, out_weight, preferred_element_type=jnp.float32)
        summed = lax.psum_scatter(partial_value, "mp", scatter_dimension=0, tiled=True)
        layer_out = (residual + summed).astype(jnp.bfloat16)
        results.append(layer_out)
        if micro_step + 1 < micro_count:
            incoming = shifted(layer_out, "section", 1)
    return jnp.stack(results)[None]


CHUNKS = 3
SWAPS = 10
DIRECT = 3


class Copies:
    def __init__(self, send_sems, recv_sems):
        self.send_sems, self.recv_sems, self.used = send_sems, recv_sems, 0

    def take(self, count):
        first = self.used
        self.used += count
        return first

    def make(self, index, source, target, device, recv=None):
        return pltpu.make_async_remote_copy(
            src_ref=source,
            dst_ref=target,
            send_sem=self.send_sems.at[index],
            recv_sem=self.recv_sems.at[index if recv is None else recv],
            device_id=device,
            device_id_type=pl.DeviceIdType.MESH,
        )


def copies_needed(steps):
    return 2 * SWAPS + 1 + 3 * CHUNKS * steps + 4 * 2 + 4 * CHUNKS * (steps - 1) + steps * CHUNKS * (4 + 3) + 2 * CHUNKS


def layer_kernel(
    steps, ctx,
    patches, carried, norm_gain, q_gain, k_gain, q_weight, k_weight, v_weight, o_weight,
    out,
    xin, before, xn, wq, wk, wv, stage, wo_t, wo, heads_first, heads_next, qkv,
    att, att_out, pair_out, pair_in, keep, far_out, far_in, fin_out, fin, crossed, outbuf,
    send_sems, recv_sems, load_sems,
):
    me_ctx = lax.axis_index("ctx")
    me_section = lax.axis_index("section")
    me_mp = lax.axis_index("mp")
    core_peer = {"mp": me_mp + 1 - 2 * lax.rem(me_mp, 2)}
    far_peer = {"mp": lax.rem(me_mp + 2, 4)}
    section_peer = {"section": 1 - me_section}
    swap_peer = {"ctx": me_ctx + 1 - 2 * lax.rem(me_ctx, 2)}
    half = lax.rem(me_ctx, 2)
    place = me_ctx // 2
    slot = 2 * half + place
    column_half = me_ctx // 2
    mirror = {"ctx": lax.rem(me_ctx + 2, ctx)}

    def ctx_at(offset):
        return lax.rem(me_ctx + offset + ctx, ctx)

    head_dim = q_gain.shape[1]
    head_count = q_weight.shape[2] // head_dim
    width = xin.shape[2]
    rows = xin.shape[1]
    chunk = rows // CHUNKS
    share = o_weight.shape[1]
    scale = math.log2(math.e) / math.sqrt(head_dim)
    first_section = me_section == 0
    last_section = me_section == 1

    patch_loads = [pltpu.make_async_copy(patches.at[t], xin.at[t], load_sems.at[t]) for t in range(steps)]
    carried_load = pltpu.make_async_copy(carried, xin.at[0], load_sems.at[0])

    @pl.when(first_section)
    def _():
        for load in patch_loads:
            load.start()

    @pl.when(last_section)
    def _():
        carried_load.start()

    head_order = [h for n in range(head_count // 2) for h in (n, head_count - 1 - n)]
    weight_loads = []
    for position, h in enumerate(head_order):
        for n, (source, target) in enumerate(((q_weight, wq), (k_weight, wk), (v_weight, wv))):
            weight_loads.append(
                pltpu.make_async_copy(
                    source.at[0, :, pl.ds(h * head_dim, head_dim)],
                    target.at[:, pl.ds(position * head_dim, head_dim)],
                    load_sems.at[2 * steps + 1 + position * 3 + n],
                )
            )
    own_columns = pl.ds(pl.multiple_of(lax.rem(me_ctx, 2) * share, 16), share)
    out_load = pltpu.make_async_copy(o_weight.at[0], wo_t.at[own_columns], load_sems.at[2 * steps])
    for load in weight_loads + [out_load]:
        load.start()

    barrier = pltpu.get_barrier_semaphore()
    peers = [core_peer, far_peer, section_peer] + [{"ctx": ctx_at(d)} for d in range(1, ctx)]
    peers += [{"ctx": ctx_at(d), "section": 1 - me_section} for d in range(1, ctx)]
    for peer in peers:
        pl.semaphore_signal(barrier, inc=1, device_id=peer, device_id_type=pl.DeviceIdType.MESH)
    pl.semaphore_wait(barrier, len(peers))

    copies = Copies(send_sems, recv_sems)
    sent = []

    base, detour_base = copies.take(SWAPS), copies.take(SWAPS)
    swaps, detours, forwards = [], [], []
    part = share // SWAPS
    for i in range(SWAPS):
        source = o_weight.at[0, pl.ds(i * part, part)]
        target = wo_t.at[pl.ds(pl.multiple_of(lax.rem(me_ctx, 2) * share + i * part, 16), part)]
        swaps.append(copies.make(base + i, source, target, swap_peer))
        if i >= DIRECT:
            between = stage.at[pl.ds(i * part, part)]
            detours.append(copies.make(detour_base + i, source, between, section_peer))
            forwards.append(
                copies.make(detour_base + i, between, target, swap_peer | {"section": 1 - me_section}, base + i)
            )
    sent += swaps[:DIRECT]
    ahead = copies.make(copies.take(1), patches.at[0], before, section_peer)

    @pl.when(first_section)
    def _():
        for detour in detours:
            detour.start()
        ahead.start()

    near, far, relay = {}, {}, {}
    for t in range(steps):
        base = copies.take(3 * CHUNKS)
        for j in range(CHUNKS):
            own = xn.at[t, 0, j, 0]
            far[t, j] = copies.make(base + j, own, xn.at[t, 1, j, 0], far_peer)
            near[t, j] = copies.make(base + CHUNKS + j, own, xn.at[t, 0, j, 1], core_peer)
            relay[t, j] = copies.make(base + 2 * CHUNKS + j, xn.at[t, 1, j, 0], xn.at[t, 1, j, 1], core_peer)
    for group in (near, far, relay):
        sent += list(group.values())

    def spread(t, j):
        values = xin[t, pl.ds(j * chunk, chunk)].astype(jnp.float32)
        xn[t, 0, j, 0] = rms_scaled(values, norm_gain[...]).astype(jnp.bfloat16)
        far[t, j].start()
        near[t, j].start()

    def project_heads(lhs, keep_part, send_part, loads=None, between=None):
        for first in range(0, head_count, 2):
            if first > 0 and between is not None:
                between()
            if loads is not None:
                for load in loads[3 * first:3 * (first + 2)]:
                    load.wait()
            lanes = pl.ds(first * head_dim, 2 * head_dim)
            raw = [jnp.dot(lhs, w[:, lanes], preferred_element_type=jnp.float32) for w in (wq, wk, wv)]
            for side in range(2):
                h = head_order[first + side]
                own = slice(side * head_dim, (side + 1) * head_dim)
                parts = [
                    rms_scaled(raw[0][:, own], q_gain[...]).astype(jnp.bfloat16),
                    rms_scaled(raw[1][:, own], k_gain[...]).astype(jnp.bfloat16),
                    raw[2][:, own].astype(jnp.bfloat16),
                ]

                @pl.when(me_ctx == h)
                def _():
                    for n in range(3):
                        keep_part(n, parts[n])

                @pl.when(me_ctx != h)
                def _():
                    for n in range(3):
                        send_part(h, n, parts[n])
                    send_part(h, None, None)

    two = 2 * chunk
    first_bases = [copies.take(ctx) for _ in range(2)]
    next_bases = [copies.take(ctx) for _ in range(CHUNKS)]

    def first_slab(g, h):
        return heads_first.at[g, h]

    def first_target(g):
        return qkv.at[0, :, :, slot, pl.ds(g * two, two)]

    def next_slab(j, h):
        return heads_next.at[j, h]

    def next_target(j):
        return qkv.at[1, :, j, slot]

    def head_of_first(g, loads=None):
        def keep_part(n, value):
            qkv[0, n, :, slot, pl.ds(g * two, two)] = value.reshape(CHUNKS, two, head_dim)

        def send_part(h, n, value):
            if n is None:
                d = lax.rem(h - me_ctx + ctx, ctx)
                copies.make(first_bases[g] + d, first_slab(g, h), first_target(g), {"ctx": h}).start()
            else:
                heads_first[g, h, n] = value.reshape(CHUNKS, two, head_dim)

        project_heads(xn[0, g].reshape(CHUNKS * two, width), keep_part, send_part, loads)

    def head_of_next_whole():
        def keep_part(n, value):
            for g in range(2):
                piece = value[g * CHUNKS * two:(g + 1) * CHUNKS * two].reshape(CHUNKS, two, head_dim)
                qkv[1, n, :, slot, pl.ds(g * two, two)] = piece

        def send_part(h, n, value):
            if n is not None:
                for g in range(2):
                    piece = value[g * CHUNKS * two:(g + 1) * CHUNKS * two].reshape(CHUNKS, two, head_dim)
                    heads_next[:, h, n, pl.ds(g * two, two)] = piece

        project_heads(xn[1].reshape(2 * CHUNKS * two, width), keep_part, send_part)

    def send_next(j):
        for d in (2, 1, ctx - 1):
            next_arrival(j, d).start()

    def next_arrival(j, d):
        return copies.make(next_bases[j] + d, next_slab(j, ctx_at(d)), next_target(j), {"ctx": ctx_at(d)})

    def head_of_next(pieces, between=None):
        def keep_part(n, value):
            for i, (g, j) in enumerate(pieces):
                qkv[1, n, j, slot, pl.ds(g * two, two)] = value[i * two:(i + 1) * two]

        def send_part(h, n, value):
            for i, (g, j) in enumerate(pieces):
                if n is None:
                    d = lax.rem(h - me_ctx + ctx, ctx)
                    part = pl.ds(g * two, two)
                    copies.make(
                        next_bases[j] + d, heads_next.at[j, h, :, part], qkv.at[1, :, j, slot, part], {"ctx": h}
                    ).start()
                else:
                    heads_next[j, h, n, pl.ds(g * two, two)] = value[i * two:(i + 1) * two]

        lhs = jnp.concatenate([xn[1, g, j].reshape(two, width) for g, j in pieces], axis=0)
        project_heads(lhs, keep_part, send_part, between=between)

    arrivals = {0: [], 1: []}
    for d in range(1, ctx):
        for g in range(2):
            arrivals[0].append(
                copies.make(first_bases[g] + d, first_slab(g, ctx_at(d)), first_target(g), {"ctx": ctx_at(d)})
            )
        for j in range(CHUNKS):
            arrivals[1].append(next_arrival(j, d))
    sent += arrivals[0] + arrivals[1]

    for swap in swaps[:DIRECT - 1]:
        swap.start()
    carried_load.wait()
    for j in range(CHUNKS):
        spread(0, j)

    @pl.when(first_section)
    def _():
        patch_loads[1].wait()
        for j in range(CHUNKS):
            spread(1, j)

    for j in range(CHUNKS):
        near[0, j].wait_recv()
    head_of_first(0, weight_loads)
    for swap in swaps[DIRECT - 1:DIRECT]:
        swap.start()

    @pl.when(last_section)
    def _():
        for detour, forward in zip(detours, forwards):
            detour.wait_recv()
            forward.start()

    for j in range(CHUNKS):
        far[0, j].wait_recv()
        relay[0, j].start()
    for j in range(CHUNKS):
        relay[0, j].wait_recv()
    head_of_first(1)

    @pl.when(first_section)
    def _():
        for j in range(CHUNKS):
            far[1, j].wait_recv()
            relay[1, j].start()

    def attend(t):
        for arrival in arrivals[t]:
            arrival.wait_recv()
        keys = qkv[t, 1].reshape(CHUNKS * 4 * ctx * chunk, head_dim)
        vals = qkv[t, 2].reshape(CHUNKS * 4 * ctx * chunk, head_dim)

        def attended(j):
            scores = lax.dot_general(
                qkv[t, 0, j].reshape(4 * ctx * chunk, head_dim), keys, (((1,), (1,)), ((), ())),
                preferred_element_type=jnp.float32,
            )
            probs = jnp.exp2(scores * scale)
            totals = jnp.sum(probs, axis=1, keepdims=True)
            weighted = jnp.dot(probs.astype(jnp.bfloat16), vals, preferred_element_type=jnp.float32)
            return (weighted / totals).astype(jnp.bfloat16)

        return attended

    def finish_rows(t, j, pieces):
        part = pl.ds(j * chunk, chunk)
        summed = jnp.concatenate(pieces, axis=1)
        return (t[part].astype(jnp.float32) + summed.astype(jnp.float32)).astype(jnp.bfloat16)

    class Tail:
        def __init__(self, t):
            self.t = t
            self.gather_base = copies.take(4 * CHUNKS)
            self.pair_base, self.far_base, self.last_base = [copies.take(CHUNKS) for _ in range(3)]

        def attend(self):
            t, base = self.t, self.gather_base
            attended = attend(t)
            for j in range(CHUNKS):
                att_out[t, j] = attended(j).reshape(2, 8 * chunk, head_dim)
                for i, (h, target) in enumerate((
                    (half, mirror), (1 - half, {"ctx": 1 - half}), (1 - half, {"ctx": 3 - half}),
                )):
                    copy = copies.make(
                        base + 4 * j + i, att_out.at[t, j, h], att.at[t, j, me_ctx], target, base + 4 * j + me_ctx
                    )
                    copy.start()
                    sent.append(copy)
                att[t, j, me_ctx] = att_out[t, j, half]
                sent.extend([self.pair(j), self.far(j), self.last(j)])

        def pair(self, j):
            return copies.make(self.pair_base + j, pair_out.at[self.t, j], pair_in.at[self.t, j], core_peer)

        def far(self, j):
            return copies.make(self.far_base + j, far_out.at[self.t, j], far_in.at[self.t, j], far_peer)

        def last(self, j):
            return copies.make(
                self.last_base + j, fin_out.at[self.t, j, 1 - place], fin.at[self.t, j, column_half], mirror
            )

        def project(self, j):
            t = self.t
            for d in range(1, ctx):
                h = ctx_at(d)
                index = self.gather_base + 4 * j
                copies.make(index, att_out.at[t, j, 0], att.at[t, j, h], mirror, index + h).wait_recv()
            lhs = jnp.concatenate([att[t, j, h] for h in range(ctx)], axis=1)
            product = jnp.dot(lhs, wo[...], preferred_element_type=jnp.float32)
            product = product.reshape(2, 4, chunk, 2 * share)
            for n in range(2):
                pair_out[t, j, n] = product[:, 2 * n + 1].astype(jnp.bfloat16)
                keep[t, j, n] = product[:, 2 * n]
            self.pair(j).start()

        def sum_pair(self, j):
            t = self.t
            self.pair(j).wait_recv()
            far_out[t, j] = (keep[t, j, 1] + pair_in[t, j, 1].astype(jnp.float32)).astype(jnp.bfloat16)
            self.far(j).start()
            keep[t, j, 0] = keep[t, j, 0] + pair_in[t, j, 0].astype(jnp.float32)

        def sum_far(self, j):
            t = self.t
            self.far(j).wait_recv()
            fin_out[t, j] = (keep[t, j, 0] + far_in[t, j].astype(jnp.float32)).astype(jnp.bfloat16)

        def spread_sum(self, j):
            t = self.t
            self.last(j).start()
            fin[t, j, column_half] = fin_out[t, j, place]

        def sum_and_spread(self, j):
            self.sum_far(j)
            self.spread_sum(j)

        def sum_and_cross(self, j):
            self.sum_far(j)
            for crossing in crossings(j, column_half):
                crossing.start()

        def finish(self, j):
            t = self.t
            self.last(j).wait_recv()
            outbuf[t, pl.ds(j * chunk, chunk)] = finish_rows(xin.at[t], j, [fin[t, j, p] for p in range(2)])

        def run(self, order):
            stages = {
                "A": self.project, "B": self.sum_pair, "C": self.sum_and_spread, "X": self.sum_and_cross,
                "L": self.spread_sum, "D": self.finish,
            }
            for name in order:
                stages[name[0]](int(name[1]))

    cross_base = copies.take(2 * CHUNKS)

    def crossings(j, sender):
        across = {"section": 1 - me_section}
        return [
            copies.make(
                cross_base + 2 * j + i, fin_out.at[0, j, p], crossed.at[j, sender], target, cross_base + 2 * j + sender
            )
            for i, (p, target) in enumerate(((1 - place, mirror | across), (place, across)))
        ]

    def take_over(j):
        for p in range(2):
            crossings(j, p)[0].wait_recv()
        xin[1, pl.ds(j * chunk, chunk)] = finish_rows(before, j, [crossed[j, p] for p in range(2)])
        spread(1, j)

    def pass_on(j):
        far[1, j].wait_recv()
        relay[1, j].start()

    def begin_next(j, between=None):
        pieces = []
        if j < CHUNKS:
            near[1, j].wait_recv()
            pieces.append((0, j))
        if j > 0:
            relay[1, j - 1].wait_recv()
            pieces.append((1, j - 1))
        head_of_next(pieces, between)

    def swap_done():
        for swap in swaps:
            swap.wait_recv()
        wo[...] = wo_t[...].T

    def store(t):
        return pltpu.make_async_copy(outbuf.at[t], out.at[0, t], load_sems.at[steps + t])

    earlier, later = Tail(0), Tail(1)
    out_load.wait()
    earlier.attend()

    @pl.when(first_section)
    def _():
        for j in range(CHUNKS):
            near[1, j].wait_recv()
            relay[1, j].wait_recv()
        head_of_next_whole()
        send_next(0)
        swap_done()
        earlier.run(["A0", "B0", "A1", "B1", "A2", "X0", "B2", "X1", "X2"])
        for j in range(1, CHUNKS):
            send_next(j)
        earlier.run(["L0", "L1", "L2"])
        earlier.run(["D0", "D1", "D2"])
        store(0).start()

    @pl.when(last_section)
    def _():
        for swap in swaps[DIRECT:]:
            swap.start()
        ahead.wait_recv()
        take_over(0)
        begin_next(0)
        take_over(1)
        pass_on(0)
        take_over(2)
        begin_next(1, functools.partial(pass_on, 1))
        begin_next(2, functools.partial(pass_on, 2))
        begin_next(3)
        swap_done()
        earlier.run(["A0", "A1", "A2", "B0", "B1", "B2"])

    later.attend()

    @pl.when(last_section)
    def _():
        earlier.run(["C0", "C1", "C2"])

    later.run(["A0", "B0", "A1", "B1", "A2", "C0", "B2", "C1", "C2"])

    @pl.when(last_section)
    def _():
        earlier.run(["D0", "D1", "D2"])
        store(0).start()

    later.run(["D0", "D1", "D2"])
    store(1).start()
    for t in range(steps):
        store(t).wait()
    for copy in sent:
        copy.wait_send()

    @pl.when(first_section)
    def _():
        for copy in detours + [ahead] + [copy for j in range(CHUNKS) for copy in crossings(j, column_half)]:
            copy.wait_send()

    @pl.when(last_section)
    def _():
        for copy in forwards + swaps[DIRECT:]:
            copy.wait_send()


def fused_device(patches, carried, norm_gain, q_gain, k_gain, q_weight, k_weight, v_weight, o_weight):
    steps, rows, width = patches.shape
    ctx = lax.axis_size("ctx")
    head_dim = q_gain.shape[1]
    columns = q_weight.shape[2]
    share = o_weight.shape[2]
    bf16, f32 = jnp.bfloat16, jnp.float32
    segment = 4 * rows
    chunk = rows // CHUNKS
    anywhere = pl.BlockSpec(memory_space=pl.ANY)
    vmem = pl.BlockSpec(memory_space=pltpu.VMEM)
    number = copies_needed(steps)
    flops = steps * 2 * segment * (3 * width * columns + ctx * columns * share + 2 * ctx * segment * columns)
    return pl.pallas_call(
        functools.partial(layer_kernel, steps, ctx),
        out_shape=jax.ShapeDtypeStruct((1, steps, rows, width), bf16),
        in_specs=[anywhere, anywhere, vmem, vmem, vmem, anywhere, anywhere, anywhere, anywhere],
        out_specs=anywhere,
        scratch_shapes=[
            pltpu.VMEM((steps, rows, width), bf16),
            pltpu.VMEM((rows, width), bf16),
            pltpu.VMEM((steps, 2, CHUNKS, 2, chunk, width), bf16),
            pltpu.VMEM((width, columns), bf16),
            pltpu.VMEM((width, columns), bf16),
            pltpu.VMEM((width, columns), bf16),
            pltpu.VMEM((share, columns), bf16),
            pltpu.VMEM((2 * share, columns), bf16),
            pltpu.VMEM((columns, 2 * share), bf16),
            pltpu.VMEM((2, ctx, 3, CHUNKS, 2 * chunk, head_dim), bf16),
            pltpu.VMEM((CHUNKS, ctx, 3, 4 * chunk, head_dim), bf16),
            pltpu.VMEM((steps, 3, CHUNKS, ctx, 4 * chunk, head_dim), bf16),
            pltpu.VMEM((steps, CHUNKS, ctx, 8 * chunk, head_dim), bf16),
            pltpu.VMEM((steps, CHUNKS, 2, 8 * chunk, head_dim), bf16),
            pltpu.VMEM((steps, CHUNKS, 2, 2, chunk, 2 * share), bf16),
            pltpu.VMEM((steps, CHUNKS, 2, 2, chunk, 2 * share), bf16),
            pltpu.VMEM((steps, CHUNKS, 2, 2, chunk, 2 * share), f32),
            pltpu.VMEM((steps, CHUNKS, 2, chunk, 2 * share), bf16),
            pltpu.VMEM((steps, CHUNKS, 2, chunk, 2 * share), bf16),
            pltpu.VMEM((steps, CHUNKS, 2, chunk, 2 * share), bf16),
            pltpu.VMEM((steps, CHUNKS, 2, chunk, 2 * share), bf16),
            pltpu.VMEM((CHUNKS, 2, chunk, 2 * share), bf16),
            pltpu.VMEM((steps, rows, width), bf16),
            pltpu.SemaphoreType.DMA((number,)),
            pltpu.SemaphoreType.DMA((number,)),
            pltpu.SemaphoreType.DMA((2 * steps + 1 + 3 * (columns // head_dim),)),
        ],
        compiler_params=pltpu.CompilerParams(
            collective_id=0, has_side_effects=True, vmem_limit_bytes=56 * 2**20
        ),
        cost_estimate=pl.CostEstimate(flops=flops, bytes_accessed=12 * 2**20, transcendentals=0),
    )(patches, carried, norm_gain, q_gain, k_gain, q_weight, k_weight, v_weight, jnp.swapaxes(o_weight, 1, 2))


def solution(mesh):
    in_specs = (
        P(None, ("ctx", "mp"), None),
        P(("ctx", "mp"), None),
        P("section", None),
        P("section", None),
        P("section", None),
        P("section", None, "mp"),
        P("section", None, "mp"),
        P("section", None, "mp"),
        P("section", "mp", "ctx"),
    )
    out_specs = P("section", None, ("ctx", "mp"), None)

    def program(*arrays):
        ctx, mp, sections = mesh.shape["ctx"], mesh.shape["mp"], mesh.shape["section"]
        heads = arrays[5].shape[2] // arrays[3].shape[1]
        rows = arrays[1].shape[0] // (ctx * mp)
        fits = mp == 4 and sections == 2 and ctx * mp == heads and ctx == 4 and rows == 16 * CHUNKS
        fits = fits and arrays[0].shape[0] == 2 and arrays[8].shape[2] % (16 * SWAPS * ctx) == 0
        body = fused_device if fits else per_device
        return jax.shard_map(body, mesh=mesh, in_specs=in_specs, out_specs=out_specs, check_vma=False)(*arrays)

    return program
```

```python
import functools
import math

import jax
import jax.numpy as jnp
from jax import lax
from jax.experimental import pallas as pl
from jax.experimental.pallas import tpu as pltpu
from jax.sharding import PartitionSpec as P

epsilon = 1e-06


def rms_scaled(values, gain):
    return values * lax.rsqrt(jnp.mean(values * values, axis=-1, keepdims=True) + epsilon) * gain


def shifted(value, axis, steps):
    count = lax.axis_size(axis)
    leading, last = (max(0, -steps), min(count, count - steps))
    return lax.ppermute(value, axis, [(source, source + steps) for source in range(leading, last)])


def per_device(patches, carried, norm_gain, q_gain, k_gain, q_weight, k_weight, v_weight, o_weight):
    micro_count = patches.shape[0]
    head_dim = q_gain.shape[1]
    head_count = q_weight.shape[2] // head_dim
    columns = head_count * head_dim
    score_scale = 1.0 / math.sqrt(head_dim)
    section_index = lax.axis_index("section")
    incoming = carried
    results = []
    out_weight = lax.all_gather(o_weight[0], "ctx", axis=1, tiled=True)
    for micro_step in range(micro_count):
        layer_input = jnp.where(section_index == 0, patches[micro_step], incoming)
        residual = layer_input.astype(jnp.float32)
        normed = rms_scaled(residual, norm_gain[0]).astype(jnp.bfloat16)
        segment = lax.all_gather(normed, "mp", axis=0, tiled=True)
        rows = segment.shape[0]
        raw_query = jnp.dot(segment, q_weight[0], preferred_element_type=jnp.float32)
        raw_key = jnp.dot(segment, k_weight[0], preferred_element_type=jnp.float32)
        raw_value = jnp.dot(segment, v_weight[0], preferred_element_type=jnp.float32)
        queries = rms_scaled(raw_query.reshape(rows, head_count, head_dim), q_gain[0])
        keys = rms_scaled(raw_key.reshape(rows, head_count, head_dim), k_gain[0])
        keys = keys.astype(jnp.bfloat16).reshape(rows, columns)
        key_block = lax.all_gather(keys, "ctx", axis=0, tiled=True)
        value_block = lax.all_gather(raw_value.astype(jnp.bfloat16), "ctx", axis=0, tiled=True)
        count = key_block.shape[0]
        scores = score_scale * jnp.einsum(
            "qhd,khd->qhk",
            queries.astype(jnp.bfloat16),
            key_block.reshape(count, head_count, head_dim),
            preferred_element_type=jnp.float32,
        )
        probs = jnp.exp(scores)
        totals = jnp.sum(probs, axis=2)
        weighted = jnp.einsum(
            "qhk,khd->qhd",
            probs.astype(jnp.bfloat16),
            value_block.reshape(count, head_count, head_dim),
            preferred_element_type=jnp.float32,
        )
        attended = (weighted / totals[:, :, None]).reshape(rows, columns).astype(jnp.bfloat16)
        partial_value = jnp.dot(attended, out_weight, preferred_element_type=jnp.float32)
        summed = lax.psum_scatter(partial_value, "mp", scatter_dimension=0, tiled=True)
        layer_out = (residual + summed).astype(jnp.bfloat16)
        results.append(layer_out)
        if micro_step + 1 < micro_count:
            incoming = shifted(layer_out, "section", 1)
    return jnp.stack(results)[None]


CHUNKS = 3
SWAPS = 10
DIRECT = 4


class Copies:
    def __init__(self, send_sems, recv_sems):
        self.send_sems, self.recv_sems, self.used = send_sems, recv_sems, 0

    def take(self, count):
        first = self.used
        self.used += count
        return first

    def make(self, index, source, target, device, recv=None):
        return pltpu.make_async_remote_copy(
            src_ref=source,
            dst_ref=target,
            send_sem=self.send_sems.at[index],
            recv_sem=self.recv_sems.at[index if recv is None else recv],
            device_id=device,
            device_id_type=pl.DeviceIdType.MESH,
        )


def copies_needed(steps):
    return 2 * SWAPS + 1 + 3 * CHUNKS * steps + 4 * 2 + 4 * CHUNKS * (steps - 1) + steps * CHUNKS * (4 + 3) + 2 * CHUNKS


def layer_kernel(
    steps, ctx,
    patches, carried, norm_gain, q_gain, k_gain, q_weight, k_weight, v_weight, o_weight,
    out,
    xin, before, xn, wq, wk, wv, stage, wo_t, wo, heads_first, heads_next, qkv,
    att, att_out, pair_out, pair_in, keep, far_out, far_in, fin_out, fin, crossed, outbuf,
    send_sems, recv_sems, load_sems,
):
    me_ctx = lax.axis_index("ctx")
    me_section = lax.axis_index("section")
    me_mp = lax.axis_index("mp")
    core_peer = {"mp": me_mp + 1 - 2 * lax.rem(me_mp, 2)}
    far_peer = {"mp": lax.rem(me_mp + 2, 4)}
    section_peer = {"section": 1 - me_section}
    swap_peer = {"ctx": me_ctx + 1 - 2 * lax.rem(me_ctx, 2)}
    half = lax.rem(me_ctx, 2)
    place = me_ctx // 2
    slot = 2 * half + place
    column_half = me_ctx // 2
    mirror = {"ctx": lax.rem(me_ctx + 2, ctx)}

    def ctx_at(offset):
        return lax.rem(me_ctx + offset + ctx, ctx)

    head_dim = q_gain.shape[1]
    head_count = q_weight.shape[2] // head_dim
    width = xin.shape[2]
    rows = xin.shape[1]
    chunk = rows // CHUNKS
    share = o_weight.shape[1]
    scale = math.log2(math.e) / math.sqrt(head_dim)
    first_section = me_section == 0
    last_section = me_section == 1

    patch_loads = [pltpu.make_async_copy(patches.at[t], xin.at[t], load_sems.at[t]) for t in range(steps)]
    carried_load = pltpu.make_async_copy(carried, xin.at[0], load_sems.at[0])

    @pl.when(first_section)
    def _():
        for load in patch_loads:
            load.start()

    @pl.when(last_section)
    def _():
        carried_load.start()

    head_order = [h for n in range(head_count // 2) for h in (n, head_count - 1 - n)]
    weight_loads = []
    for position, h in enumerate(head_order):
        for n, (source, target) in enumerate(((q_weight, wq), (k_weight, wk), (v_weight, wv))):
            weight_loads.append(
                pltpu.make_async_copy(
                    source.at[0, :, pl.ds(h * head_dim, head_dim)],
                    target.at[:, pl.ds(position * head_dim, head_dim)],
                    load_sems.at[2 * steps + 1 + position * 3 + n],
                )
            )
    own_columns = pl.ds(pl.multiple_of(lax.rem(me_ctx, 2) * share, 16), share)
    out_load = pltpu.make_async_copy(o_weight.at[0], wo_t.at[own_columns], load_sems.at[2 * steps])
    for load in weight_loads + [out_load]:
        load.start()

    barrier = pltpu.get_barrier_semaphore()
    peers = [core_peer, far_peer, section_peer] + [{"ctx": ctx_at(d)} for d in range(1, ctx)]
    peers += [{"ctx": ctx_at(d), "section": 1 - me_section} for d in range(1, ctx)]
    for peer in peers:
        pl.semaphore_signal(barrier, inc=1, device_id=peer, device_id_type=pl.DeviceIdType.MESH)
    pl.semaphore_wait(barrier, len(peers))

    copies = Copies(send_sems, recv_sems)
    sent = []

    base, detour_base = copies.take(SWAPS), copies.take(SWAPS)
    swaps, detours, forwards = [], [], []
    part = share // SWAPS
    for i in range(SWAPS):
        source = o_weight.at[0, pl.ds(i * part, part)]
        target = wo_t.at[pl.ds(pl.multiple_of(lax.rem(me_ctx, 2) * share + i * part, 16), part)]
        swaps.append(copies.make(base + i, source, target, swap_peer))
        if i >= DIRECT:
            between = stage.at[pl.ds(i * part, part)]
            detours.append(copies.make(detour_base + i, source, between, section_peer))
            forwards.append(
                copies.make(detour_base + i, between, target, swap_peer | {"section": 1 - me_section}, base + i)
            )
    sent += swaps[:DIRECT]
    ahead = copies.make(copies.take(1), patches.at[0], before, section_peer)

    @pl.when(first_section)
    def _():
        for detour in detours:
            detour.start()
        ahead.start()

    near, far, relay = {}, {}, {}
    for t in range(steps):
        base = copies.take(3 * CHUNKS)
        for j in range(CHUNKS):
            own = xn.at[t, 0, j, 0]
            far[t, j] = copies.make(base + j, own, xn.at[t, 1, j, 0], far_peer)
            near[t, j] = copies.make(base + CHUNKS + j, own, xn.at[t, 0, j, 1], core_peer)
            relay[t, j] = copies.make(base + 2 * CHUNKS + j, xn.at[t, 1, j, 0], xn.at[t, 1, j, 1], core_peer)
    for group in (near, far, relay):
        sent += list(group.values())

    def spread(t, j):
        values = xin[t, pl.ds(j * chunk, chunk)].astype(jnp.float32)
        xn[t, 0, j, 0] = rms_scaled(values, norm_gain[...]).astype(jnp.bfloat16)
        far[t, j].start()
        near[t, j].start()

    def project_heads(lhs, keep_part, send_part, loads=None, between=None):
        for first in range(0, head_count, 2):
            if first > 0 and between is not None:
                between()
            if loads is not None:
                for load in loads[3 * first:3 * (first + 2)]:
                    load.wait()
            lanes = pl.ds(first * head_dim, 2 * head_dim)
            raw = [jnp.dot(lhs, w[:, lanes], preferred_element_type=jnp.float32) for w in (wq, wk, wv)]
            for side in range(2):
                h = head_order[first + side]
                own = slice(side * head_dim, (side + 1) * head_dim)
                parts = [
                    rms_scaled(raw[0][:, own], q_gain[...]).astype(jnp.bfloat16),
                    rms_scaled(raw[1][:, own], k_gain[...]).astype(jnp.bfloat16),
                    raw[2][:, own].astype(jnp.bfloat16),
                ]

                @pl.when(me_ctx == h)
                def _():
                    for n in range(3):
                        keep_part(n, parts[n])

                @pl.when(me_ctx != h)
                def _():
                    for n in range(3):
                        send_part(h, n, parts[n])
                    send_part(h, None, None)

    two = 2 * chunk
    first_bases = [copies.take(ctx) for _ in range(2)]
    next_bases = [copies.take(ctx) for _ in range(CHUNKS)]

    def first_slab(g, h):
        return heads_first.at[g, h]

    def first_target(g):
        return qkv.at[0, :, :, slot, pl.ds(g * two, two)]

    def next_slab(j, h):
        return heads_next.at[j, h]

    def next_target(j):
        return qkv.at[1, :, j, slot]

    def head_of_first(g, loads=None):
        def keep_part(n, value):
            qkv[0, n, :, slot, pl.ds(g * two, two)] = value.reshape(CHUNKS, two, head_dim)

        def send_part(h, n, value):
            if n is None:
                d = lax.rem(h - me_ctx + ctx, ctx)
                copies.make(first_bases[g] + d, first_slab(g, h), first_target(g), {"ctx": h}).start()
            else:
                heads_first[g, h, n] = value.reshape(CHUNKS, two, head_dim)

        project_heads(xn[0, g].reshape(CHUNKS * two, width), keep_part, send_part, loads)

    def head_of_next_whole():
        def keep_part(n, value):
            for g in range(2):
                piece = value[g * CHUNKS * two:(g + 1) * CHUNKS * two].reshape(CHUNKS, two, head_dim)
                qkv[1, n, :, slot, pl.ds(g * two, two)] = piece

        def send_part(h, n, value):
            if n is not None:
                for g in range(2):
                    piece = value[g * CHUNKS * two:(g + 1) * CHUNKS * two].reshape(CHUNKS, two, head_dim)
                    heads_next[:, h, n, pl.ds(g * two, two)] = piece

        project_heads(xn[1].reshape(2 * CHUNKS * two, width), keep_part, send_part)

    def send_next(j):
        for d in (2, 1, ctx - 1):
            next_arrival(j, d).start()

    def next_arrival(j, d):
        return copies.make(next_bases[j] + d, next_slab(j, ctx_at(d)), next_target(j), {"ctx": ctx_at(d)})

    def head_of_next(pieces, between=None):
        def keep_part(n, value):
            for i, (g, j) in enumerate(pieces):
                qkv[1, n, j, slot, pl.ds(g * two, two)] = value[i * two:(i + 1) * two]

        def send_part(h, n, value):
            for i, (g, j) in enumerate(pieces):
                if n is None:
                    d = lax.rem(h - me_ctx + ctx, ctx)
                    part = pl.ds(g * two, two)
                    copies.make(
                        next_bases[j] + d, heads_next.at[j, h, :, part], qkv.at[1, :, j, slot, part], {"ctx": h}
                    ).start()
                else:
                    heads_next[j, h, n, pl.ds(g * two, two)] = value[i * two:(i + 1) * two]

        lhs = jnp.concatenate([xn[1, g, j].reshape(two, width) for g, j in pieces], axis=0)
        project_heads(lhs, keep_part, send_part, between=between)

    arrivals = {0: [], 1: []}
    for d in range(1, ctx):
        for g in range(2):
            arrivals[0].append(
                copies.make(first_bases[g] + d, first_slab(g, ctx_at(d)), first_target(g), {"ctx": ctx_at(d)})
            )
        for j in range(CHUNKS):
            arrivals[1].append(next_arrival(j, d))
    sent += arrivals[0] + arrivals[1]

    for swap in swaps[:2]:
        swap.start()
    carried_load.wait()
    for j in range(CHUNKS):
        spread(0, j)

    @pl.when(first_section)
    def _():
        patch_loads[1].wait()
        for j in range(CHUNKS):
            spread(1, j)

    for j in range(CHUNKS):
        near[0, j].wait_recv()
    head_of_first(0, weight_loads)
    for swap in swaps[2:DIRECT]:
        swap.start()

    @pl.when(last_section)
    def _():
        for detour, forward in zip(detours, forwards):
            detour.wait_recv()
            forward.start()

    for j in range(CHUNKS):
        far[0, j].wait_recv()
        relay[0, j].start()
    for j in range(CHUNKS):
        relay[0, j].wait_recv()
    head_of_first(1)

    @pl.when(first_section)
    def _():
        for j in range(CHUNKS):
            far[1, j].wait_recv()
            relay[1, j].start()

    def attend(t):
        for arrival in arrivals[t]:
            arrival.wait_recv()
        keys = qkv[t, 1].reshape(CHUNKS * 4 * ctx * chunk, head_dim)
        vals = qkv[t, 2].reshape(CHUNKS * 4 * ctx * chunk, head_dim)

        def attended(j):
            scores = lax.dot_general(
                qkv[t, 0, j].reshape(4 * ctx * chunk, head_dim), keys, (((1,), (1,)), ((), ())),
                preferred_element_type=jnp.float32,
            )
            probs = jnp.exp2(scores * scale)
            totals = jnp.sum(probs, axis=1, keepdims=True)
            weighted = jnp.dot(probs.astype(jnp.bfloat16), vals, preferred_element_type=jnp.float32)
            return (weighted / totals).astype(jnp.bfloat16)

        return attended

    def finish_rows(t, j, pieces):
        part = pl.ds(j * chunk, chunk)
        summed = jnp.concatenate(pieces, axis=1)
        return (t[part].astype(jnp.float32) + summed.astype(jnp.float32)).astype(jnp.bfloat16)

    class Tail:
        def __init__(self, t):
            self.t = t
            self.gather_base = copies.take(4 * CHUNKS)
            self.pair_base, self.far_base, self.last_base = [copies.take(CHUNKS) for _ in range(3)]

        def attend(self):
            t, base = self.t, self.gather_base
            attended = attend(t)
            for j in range(CHUNKS):
                att_out[t, j] = attended(j).reshape(2, 8 * chunk, head_dim)
                for i, (h, target) in enumerate((
                    (half, mirror), (1 - half, {"ctx": 1 - half}), (1 - half, {"ctx": 3 - half}),
                )):
                    copy = copies.make(
                        base + 4 * j + i, att_out.at[t, j, h], att.at[t, j, me_ctx], target, base + 4 * j + me_ctx
                    )
                    copy.start()
                    sent.append(copy)
                att[t, j, me_ctx] = att_out[t, j, half]
                sent.extend([self.pair(j), self.far(j), self.last(j)])

        def pair(self, j):
            return copies.make(self.pair_base + j, pair_out.at[self.t, j], pair_in.at[self.t, j], core_peer)

        def far(self, j):
            return copies.make(self.far_base + j, far_out.at[self.t, j], far_in.at[self.t, j], far_peer)

        def last(self, j):
            return copies.make(
                self.last_base + j, fin_out.at[self.t, j, 1 - place], fin.at[self.t, j, column_half], mirror
            )

        def project(self, j):
            t = self.t
            for d in range(1, ctx):
                h = ctx_at(d)
                index = self.gather_base + 4 * j
                copies.make(index, att_out.at[t, j, 0], att.at[t, j, h], mirror, index + h).wait_recv()
            lhs = jnp.concatenate([att[t, j, h] for h in range(ctx)], axis=1)
            product = jnp.dot(lhs, wo[...], preferred_element_type=jnp.float32)
            product = product.reshape(2, 4, chunk, 2 * share)
            for n in range(2):
                pair_out[t, j, n] = product[:, 2 * n + 1].astype(jnp.bfloat16)
                keep[t, j, n] = product[:, 2 * n]
            self.pair(j).start()

        def sum_pair(self, j):
            t = self.t
            self.pair(j).wait_recv()
            far_out[t, j] = (keep[t, j, 1] + pair_in[t, j, 1].astype(jnp.float32)).astype(jnp.bfloat16)
            self.far(j).start()
            keep[t, j, 0] = keep[t, j, 0] + pair_in[t, j, 0].astype(jnp.float32)

        def sum_far(self, j):
            t = self.t
            self.far(j).wait_recv()
            fin_out[t, j] = (keep[t, j, 0] + far_in[t, j].astype(jnp.float32)).astype(jnp.bfloat16)

        def spread_sum(self, j):
            t = self.t
            self.last(j).start()
            fin[t, j, column_half] = fin_out[t, j, place]

        def sum_and_spread(self, j):
            self.sum_far(j)
            self.spread_sum(j)

        def sum_and_cross(self, j):
            self.sum_far(j)
            for crossing in crossings(j, column_half):
                crossing.start()

        def finish(self, j):
            t = self.t
            self.last(j).wait_recv()
            outbuf[t, pl.ds(j * chunk, chunk)] = finish_rows(xin.at[t], j, [fin[t, j, p] for p in range(2)])

        def run(self, order):
            stages = {
                "A": self.project, "B": self.sum_pair, "C": self.sum_and_spread, "X": self.sum_and_cross,
                "L": self.spread_sum, "D": self.finish,
            }
            for name in order:
                stages[name[0]](int(name[1]))

    cross_base = copies.take(2 * CHUNKS)

    def crossings(j, sender):
        across = {"section": 1 - me_section}
        return [
            copies.make(
                cross_base + 2 * j + i, fin_out.at[0, j, p], crossed.at[j, sender], target, cross_base + 2 * j + sender
            )
            for i, (p, target) in enumerate(((1 - place, mirror | across), (place, across)))
        ]

    def take_over(j):
        for p in range(2):
            crossings(j, p)[0].wait_recv()
        xin[1, pl.ds(j * chunk, chunk)] = finish_rows(before, j, [crossed[j, p] for p in range(2)])
        spread(1, j)

    def pass_on(j):
        far[1, j].wait_recv()
        relay[1, j].start()

    def begin_next(j, between=None):
        pieces = []
        if j < CHUNKS:
            near[1, j].wait_recv()
            pieces.append((0, j))
        if j > 0:
            relay[1, j - 1].wait_recv()
            pieces.append((1, j - 1))
        head_of_next(pieces, between)

    def swap_done():
        for swap in swaps:
            swap.wait_recv()
        wo[...] = wo_t[...].T

    def store(t):
        return pltpu.make_async_copy(outbuf.at[t], out.at[0, t], load_sems.at[steps + t])

    earlier, later = Tail(0), Tail(1)
    out_load.wait()
    earlier.attend()

    @pl.when(first_section)
    def _():
        for j in range(CHUNKS):
            near[1, j].wait_recv()
            relay[1, j].wait_recv()
        head_of_next_whole()
        send_next(0)
        swap_done()
        earlier.run(["A0", "B0", "A1", "B1", "A2", "X0", "B2", "X1", "X2"])
        for j in range(1, CHUNKS):
            send_next(j)
        earlier.run(["L0", "L1", "L2"])
        earlier.run(["D0", "D1", "D2"])
        store(0).start()

    @pl.when(last_section)
    def _():
        for swap in swaps[DIRECT:]:
            swap.start()
        ahead.wait_recv()
        take_over(0)
        begin_next(0)
        take_over(1)
        pass_on(0)
        take_over(2)
        begin_next(1, functools.partial(pass_on, 1))
        begin_next(2, functools.partial(pass_on, 2))
        begin_next(3)
        swap_done()
        earlier.run(["A0", "A1", "B0", "A2", "B1", "B2"])

    later.attend()

    @pl.when(last_section)
    def _():
        earlier.run(["C0", "C1"])

    later.run(["A0"])

    @pl.when(last_section)
    def _():
        earlier.run(["C2"])

    later.run(["B0", "A1", "B1", "A2", "C0", "B2", "C1", "C2"])

    @pl.when(last_section)
    def _():
        earlier.run(["D0", "D1", "D2"])
        store(0).start()

    later.run(["D0", "D1", "D2"])
    store(1).start()
    for t in range(steps):
        store(t).wait()
    for copy in sent:
        copy.wait_send()

    @pl.when(first_section)
    def _():
        for copy in detours + [ahead] + [copy for j in range(CHUNKS) for copy in crossings(j, column_half)]:
            copy.wait_send()

    @pl.when(last_section)
    def _():
        for copy in forwards + swaps[DIRECT:]:
            copy.wait_send()


def fused_device(patches, carried, norm_gain, q_gain, k_gain, q_weight, k_weight, v_weight, o_weight):
    steps, rows, width = patches.shape
    ctx = lax.axis_size("ctx")
    head_dim = q_gain.shape[1]
    columns = q_weight.shape[2]
    share = o_weight.shape[2]
    bf16, f32 = jnp.bfloat16, jnp.float32
    segment = 4 * rows
    chunk = rows // CHUNKS
    anywhere = pl.BlockSpec(memory_space=pl.ANY)
    vmem = pl.BlockSpec(memory_space=pltpu.VMEM)
    number = copies_needed(steps)
    flops = steps * 2 * segment * (3 * width * columns + ctx * columns * share + 2 * ctx * segment * columns)
    return pl.pallas_call(
        functools.partial(layer_kernel, steps, ctx),
        out_shape=jax.ShapeDtypeStruct((1, steps, rows, width), bf16),
        in_specs=[anywhere, anywhere, vmem, vmem, vmem, anywhere, anywhere, anywhere, anywhere],
        out_specs=anywhere,
        scratch_shapes=[
            pltpu.VMEM((steps, rows, width), bf16),
            pltpu.VMEM((rows, width), bf16),
            pltpu.VMEM((steps, 2, CHUNKS, 2, chunk, width), bf16),
            pltpu.VMEM((width, columns), bf16),
            pltpu.VMEM((width, columns), bf16),
            pltpu.VMEM((width, columns), bf16),
            pltpu.VMEM((share, columns), bf16),
            pltpu.VMEM((2 * share, columns), bf16),
            pltpu.VMEM((columns, 2 * share), bf16),
            pltpu.VMEM((2, ctx, 3, CHUNKS, 2 * chunk, head_dim), bf16),
            pltpu.VMEM((CHUNKS, ctx, 3, 4 * chunk, head_dim), bf16),
            pltpu.VMEM((steps, 3, CHUNKS, ctx, 4 * chunk, head_dim), bf16),
            pltpu.VMEM((steps, CHUNKS, ctx, 8 * chunk, head_dim), bf16),
            pltpu.VMEM((steps, CHUNKS, 2, 8 * chunk, head_dim), bf16),
            pltpu.VMEM((steps, CHUNKS, 2, 2, chunk, 2 * share), bf16),
            pltpu.VMEM((steps, CHUNKS, 2, 2, chunk, 2 * share), bf16),
            pltpu.VMEM((steps, CHUNKS, 2, 2, chunk, 2 * share), f32),
            pltpu.VMEM((steps, CHUNKS, 2, chunk, 2 * share), bf16),
            pltpu.VMEM((steps, CHUNKS, 2, chunk, 2 * share), bf16),
            pltpu.VMEM((steps, CHUNKS, 2, chunk, 2 * share), bf16),
            pltpu.VMEM((steps, CHUNKS, 2, chunk, 2 * share), bf16),
            pltpu.VMEM((CHUNKS, 2, chunk, 2 * share), bf16),
            pltpu.VMEM((steps, rows, width), bf16),
            pltpu.SemaphoreType.DMA((number,)),
            pltpu.SemaphoreType.DMA((number,)),
            pltpu.SemaphoreType.DMA((2 * steps + 1 + 3 * (columns // head_dim),)),
        ],
        compiler_params=pltpu.CompilerParams(
            collective_id=0, has_side_effects=True, vmem_limit_bytes=56 * 2**20
        ),
        cost_estimate=pl.CostEstimate(flops=flops, bytes_accessed=12 * 2**20, transcendentals=0),
    )(patches, carried, norm_gain, q_gain, k_gain, q_weight, k_weight, v_weight, jnp.swapaxes(o_weight, 1, 2))


def solution(mesh):
    in_specs = (
        P(None, ("ctx", "mp"), None),
        P(("ctx", "mp"), None),
        P("section", None),
        P("section", None),
        P("section", None),
        P("section", None, "mp"),
        P("section", None, "mp"),
        P("section", None, "mp"),
        P("section", "mp", "ctx"),
    )
    out_specs = P("section", None, ("ctx", "mp"), None)

    def program(*arrays):
        ctx, mp, sections = mesh.shape["ctx"], mesh.shape["mp"], mesh.shape["section"]
        heads = arrays[5].shape[2] // arrays[3].shape[1]
        rows = arrays[1].shape[0] // (ctx * mp)
        fits = mp == 4 and sections == 2 and ctx * mp == heads and ctx == 4 and rows == 16 * CHUNKS
        fits = fits and arrays[0].shape[0] == 2 and arrays[8].shape[2] % (16 * SWAPS * ctx) == 0
        body = fused_device if fits else per_device
        return jax.shard_map(body, mesh=mesh, in_specs=in_specs, out_specs=out_specs, check_vma=False)(*arrays)

    return program
```

```python
import functools
import math

import jax
import jax.numpy as jnp
from jax import lax
from jax.experimental import pallas as pl
from jax.experimental.pallas import tpu as pltpu
from jax.sharding import PartitionSpec as P

epsilon = 1e-06


def rms_scaled(values, gain):
    return values * lax.rsqrt(jnp.mean(values * values, axis=-1, keepdims=True) + epsilon) * gain


def shifted(value, axis, steps):
    count = lax.axis_size(axis)
    leading, last = (max(0, -steps), min(count, count - steps))
    return lax.ppermute(value, axis, [(source, source + steps) for source in range(leading, last)])


def per_device(patches, carried, norm_gain, q_gain, k_gain, q_weight, k_weight, v_weight, o_weight):
    micro_count = patches.shape[0]
    head_dim = q_gain.shape[1]
    head_count = q_weight.shape[2] // head_dim
    columns = head_count * head_dim
    score_scale = 1.0 / math.sqrt(head_dim)
    section_index = lax.axis_index("section")
    incoming = carried
    results = []
    out_weight = lax.all_gather(o_weight[0], "ctx", axis=1, tiled=True)
    for micro_step in range(micro_count):
        layer_input = jnp.where(section_index == 0, patches[micro_step], incoming)
        residual = layer_input.astype(jnp.float32)
        normed = rms_scaled(residual, norm_gain[0]).astype(jnp.bfloat16)
        segment = lax.all_gather(normed, "mp", axis=0, tiled=True)
        rows = segment.shape[0]
        raw_query = jnp.dot(segment, q_weight[0], preferred_element_type=jnp.float32)
        raw_key = jnp.dot(segment, k_weight[0], preferred_element_type=jnp.float32)
        raw_value = jnp.dot(segment, v_weight[0], preferred_element_type=jnp.float32)
        queries = rms_scaled(raw_query.reshape(rows, head_count, head_dim), q_gain[0])
        keys = rms_scaled(raw_key.reshape(rows, head_count, head_dim), k_gain[0])
        keys = keys.astype(jnp.bfloat16).reshape(rows, columns)
        key_block = lax.all_gather(keys, "ctx", axis=0, tiled=True)
        value_block = lax.all_gather(raw_value.astype(jnp.bfloat16), "ctx", axis=0, tiled=True)
        count = key_block.shape[0]
        scores = score_scale * jnp.einsum(
            "qhd,khd->qhk",
            queries.astype(jnp.bfloat16),
            key_block.reshape(count, head_count, head_dim),
            preferred_element_type=jnp.float32,
        )
        probs = jnp.exp(scores)
        totals = jnp.sum(probs, axis=2)
        weighted = jnp.einsum(
            "qhk,khd->qhd",
            probs.astype(jnp.bfloat16),
            value_block.reshape(count, head_count, head_dim),
            preferred_element_type=jnp.float32,
        )
        attended = (weighted / totals[:, :, None]).reshape(rows, columns).astype(jnp.bfloat16)
        partial_value = jnp.dot(attended, out_weight, preferred_element_type=jnp.float32)
        summed = lax.psum_scatter(partial_value, "mp", scatter_dimension=0, tiled=True)
        layer_out = (residual + summed).astype(jnp.bfloat16)
        results.append(layer_out)
        if micro_step + 1 < micro_count:
            incoming = shifted(layer_out, "section", 1)
    return jnp.stack(results)[None]


CHUNKS = 3
SWAPS = 10
DIRECT = 4


class Copies:
    def __init__(self, send_sems, recv_sems):
        self.send_sems, self.recv_sems, self.used = send_sems, recv_sems, 0

    def take(self, count):
        first = self.used
        self.used += count
        return first

    def make(self, index, source, target, device, recv=None):
        return pltpu.make_async_remote_copy(
            src_ref=source,
            dst_ref=target,
            send_sem=self.send_sems.at[index],
            recv_sem=self.recv_sems.at[index if recv is None else recv],
            device_id=device,
            device_id_type=pl.DeviceIdType.MESH,
        )


def copies_needed(steps):
    return 2 * SWAPS + 1 + 3 * CHUNKS * steps + 4 * 2 + 4 * CHUNKS * (steps - 1) + steps * CHUNKS * (4 + 3) + 2 * CHUNKS


def layer_kernel(
    steps, ctx,
    patches, carried, norm_gain, q_gain, k_gain, q_weight, k_weight, v_weight, o_weight,
    out,
    xin, before, xn, wq, wk, wv, stage, wo_t, wo, heads_first, heads_next, qkv,
    att, att_out, pair_out, pair_in, keep, far_out, far_in, fin_out, fin, crossed, outbuf,
    send_sems, recv_sems, load_sems,
):
    me_ctx = lax.axis_index("ctx")
    me_section = lax.axis_index("section")
    me_mp = lax.axis_index("mp")
    core_peer = {"mp": me_mp + 1 - 2 * lax.rem(me_mp, 2)}
    far_peer = {"mp": lax.rem(me_mp + 2, 4)}
    section_peer = {"section": 1 - me_section}
    swap_peer = {"ctx": me_ctx + 1 - 2 * lax.rem(me_ctx, 2)}
    half = lax.rem(me_ctx, 2)
    place = me_ctx // 2
    slot = 2 * half + place
    column_half = me_ctx // 2
    mirror = {"ctx": lax.rem(me_ctx + 2, ctx)}

    def ctx_at(offset):
        return lax.rem(me_ctx + offset + ctx, ctx)

    head_dim = q_gain.shape[1]
    head_count = q_weight.shape[2] // head_dim
    width = xin.shape[2]
    rows = xin.shape[1]
    chunk = rows // CHUNKS
    share = o_weight.shape[1]
    scale = math.log2(math.e) / math.sqrt(head_dim)
    first_section = me_section == 0
    last_section = me_section == 1

    patch_loads = [pltpu.make_async_copy(patches.at[t], xin.at[t], load_sems.at[t]) for t in range(steps)]
    carried_load = pltpu.make_async_copy(carried, xin.at[0], load_sems.at[0])

    @pl.when(first_section)
    def _():
        for load in patch_loads:
            load.start()

    @pl.when(last_section)
    def _():
        carried_load.start()

    head_order = [h for n in range(head_count // 2) for h in (n, head_count - 1 - n)]
    weight_loads = []
    for position, h in enumerate(head_order):
        for n, (source, target) in enumerate(((q_weight, wq), (k_weight, wk), (v_weight, wv))):
            weight_loads.append(
                pltpu.make_async_copy(
                    source.at[0, :, pl.ds(h * head_dim, head_dim)],
                    target.at[:, pl.ds(position * head_dim, head_dim)],
                    load_sems.at[2 * steps + 1 + position * 3 + n],
                )
            )
    own_columns = pl.ds(pl.multiple_of(lax.rem(me_ctx, 2) * share, 16), share)
    out_load = pltpu.make_async_copy(o_weight.at[0], wo_t.at[own_columns], load_sems.at[2 * steps])
    for load in weight_loads + [out_load]:
        load.start()

    barrier = pltpu.get_barrier_semaphore()
    peers = [core_peer, far_peer, section_peer] + [{"ctx": ctx_at(d)} for d in range(1, ctx)]
    peers += [{"ctx": ctx_at(d), "section": 1 - me_section} for d in range(1, ctx)]
    for peer in peers:
        pl.semaphore_signal(barrier, inc=1, device_id=peer, device_id_type=pl.DeviceIdType.MESH)
    pl.semaphore_wait(barrier, len(peers))

    copies = Copies(send_sems, recv_sems)
    sent = []

    base, detour_base = copies.take(SWAPS), copies.take(SWAPS)
    swaps, detours, forwards = [], [], []
    part = share // SWAPS
    for i in range(SWAPS):
        source = o_weight.at[0, pl.ds(i * part, part)]
        target = wo_t.at[pl.ds(pl.multiple_of(lax.rem(me_ctx, 2) * share + i * part, 16), part)]
        swaps.append(copies.make(base + i, source, target, swap_peer))
        if i >= DIRECT:
            between = stage.at[pl.ds(i * part, part)]
            detours.append(copies.make(detour_base + i, source, between, section_peer))
            forwards.append(
                copies.make(detour_base + i, between, target, swap_peer | {"section": 1 - me_section}, base + i)
            )
    sent += swaps[:DIRECT]
    ahead = copies.make(copies.take(1), patches.at[0], before, section_peer)

    @pl.when(first_section)
    def _():
        for detour in detours:
            detour.start()
        ahead.start()

    near, far, relay = {}, {}, {}
    for t in range(steps):
        base = copies.take(3 * CHUNKS)
        for j in range(CHUNKS):
            own = xn.at[t, 0, j, 0]
            far[t, j] = copies.make(base + j, own, xn.at[t, 1, j, 0], far_peer)
            near[t, j] = copies.make(base + CHUNKS + j, own, xn.at[t, 0, j, 1], core_peer)
            relay[t, j] = copies.make(base + 2 * CHUNKS + j, xn.at[t, 1, j, 0], xn.at[t, 1, j, 1], core_peer)
    for group in (near, far, relay):
        sent += list(group.values())

    def spread(t, j):
        values = xin[t, pl.ds(j * chunk, chunk)].astype(jnp.float32)
        xn[t, 0, j, 0] = rms_scaled(values, norm_gain[...]).astype(jnp.bfloat16)
        far[t, j].start()
        near[t, j].start()

    def project_heads(lhs, keep_part, send_part, loads=None, between=None):
        for first in range(0, head_count, 2):
            if first > 0 and between is not None:
                between()
            if loads is not None:
                for load in loads[3 * first:3 * (first + 2)]:
                    load.wait()
            lanes = pl.ds(first * head_dim, 2 * head_dim)
            raw = [jnp.dot(lhs, w[:, lanes], preferred_element_type=jnp.float32) for w in (wq, wk, wv)]
            for side in range(2):
                h = head_order[first + side]
                own = slice(side * head_dim, (side + 1) * head_dim)
                parts = [
                    rms_scaled(raw[0][:, own], q_gain[...]).astype(jnp.bfloat16),
                    rms_scaled(raw[1][:, own], k_gain[...]).astype(jnp.bfloat16),
                    raw[2][:, own].astype(jnp.bfloat16),
                ]

                @pl.when(me_ctx == h)
                def _():
                    for n in range(3):
                        keep_part(n, parts[n])

                @pl.when(me_ctx != h)
                def _():
                    for n in range(3):
                        send_part(h, n, parts[n])
                    send_part(h, None, None)

    two = 2 * chunk
    first_bases = [copies.take(ctx) for _ in range(2)]
    next_bases = [copies.take(ctx) for _ in range(CHUNKS)]

    def first_slab(g, h):
        return heads_first.at[g, h]

    def first_target(g):
        return qkv.at[0, :, :, slot, pl.ds(g * two, two)]

    def next_slab(j, h):
        return heads_next.at[j, h]

    def next_target(j):
        return qkv.at[1, :, j, slot]

    def head_of_first(g, loads=None):
        def keep_part(n, value):
            qkv[0, n, :, slot, pl.ds(g * two, two)] = value.reshape(CHUNKS, two, head_dim)

        def send_part(h, n, value):
            if n is None:
                d = lax.rem(h - me_ctx + ctx, ctx)
                copies.make(first_bases[g] + d, first_slab(g, h), first_target(g), {"ctx": h}).start()
            else:
                heads_first[g, h, n] = value.reshape(CHUNKS, two, head_dim)

        project_heads(xn[0, g].reshape(CHUNKS * two, width), keep_part, send_part, loads)

    def head_of_next_whole():
        def keep_part(n, value):
            for g in range(2):
                piece = value[g * CHUNKS * two:(g + 1) * CHUNKS * two].reshape(CHUNKS, two, head_dim)
                qkv[1, n, :, slot, pl.ds(g * two, two)] = piece

        def send_part(h, n, value):
            if n is not None:
                for g in range(2):
                    piece = value[g * CHUNKS * two:(g + 1) * CHUNKS * two].reshape(CHUNKS, two, head_dim)
                    heads_next[:, h, n, pl.ds(g * two, two)] = piece

        project_heads(xn[1].reshape(2 * CHUNKS * two, width), keep_part, send_part)

    def send_next(j):
        for d in (2, 1, ctx - 1):
            next_arrival(j, d).start()

    def next_arrival(j, d):
        return copies.make(next_bases[j] + d, next_slab(j, ctx_at(d)), next_target(j), {"ctx": ctx_at(d)})

    def head_of_next(pieces, between=None):
        def keep_part(n, value):
            for i, (g, j) in enumerate(pieces):
                qkv[1, n, j, slot, pl.ds(g * two, two)] = value[i * two:(i + 1) * two]

        def send_part(h, n, value):
            for i, (g, j) in enumerate(pieces):
                if n is None:
                    d = lax.rem(h - me_ctx + ctx, ctx)
                    part = pl.ds(g * two, two)
                    copies.make(
                        next_bases[j] + d, heads_next.at[j, h, :, part], qkv.at[1, :, j, slot, part], {"ctx": h}
                    ).start()
                else:
                    heads_next[j, h, n, pl.ds(g * two, two)] = value[i * two:(i + 1) * two]

        lhs = jnp.concatenate([xn[1, g, j].reshape(two, width) for g, j in pieces], axis=0)
        project_heads(lhs, keep_part, send_part, between=between)

    arrivals = {0: [], 1: []}
    for d in range(1, ctx):
        for g in range(2):
            arrivals[0].append(
                copies.make(first_bases[g] + d, first_slab(g, ctx_at(d)), first_target(g), {"ctx": ctx_at(d)})
            )
        for j in range(CHUNKS):
            arrivals[1].append(next_arrival(j, d))
    sent += arrivals[0] + arrivals[1]

    for swap in swaps[:2]:
        swap.start()
    carried_load.wait()
    for j in range(CHUNKS):
        spread(0, j)

    for j in range(CHUNKS):
        near[0, j].wait_recv()
    head_of_first(0, weight_loads)
    for swap in swaps[2:DIRECT]:
        swap.start()

    @pl.when(first_section)
    def _():
        patch_loads[1].wait()
        for j in range(CHUNKS):
            spread(1, j)

    @pl.when(last_section)
    def _():
        for detour, forward in zip(detours, forwards):
            detour.wait_recv()
            forward.start()

    for j in range(CHUNKS):
        far[0, j].wait_recv()
        relay[0, j].start()
    for j in range(CHUNKS):
        relay[0, j].wait_recv()
    head_of_first(1)

    @pl.when(first_section)
    def _():
        for j in range(CHUNKS):
            far[1, j].wait_recv()
            relay[1, j].start()

    def attend(t):
        for arrival in arrivals[t]:
            arrival.wait_recv()
        keys = qkv[t, 1].reshape(CHUNKS * 4 * ctx * chunk, head_dim)
        vals = qkv[t, 2].reshape(CHUNKS * 4 * ctx * chunk, head_dim)

        def attended(j):
            scores = lax.dot_general(
                qkv[t, 0, j].reshape(4 * ctx * chunk, head_dim), keys, (((1,), (1,)), ((), ())),
                preferred_element_type=jnp.float32,
            )
            probs = jnp.exp2(scores * scale)
            totals = jnp.sum(probs, axis=1, keepdims=True)
            weighted = jnp.dot(probs.astype(jnp.bfloat16), vals, preferred_element_type=jnp.float32)
            return (weighted / totals).astype(jnp.bfloat16)

        return attended

    def finish_rows(t, j, pieces):
        part = pl.ds(j * chunk, chunk)
        summed = jnp.concatenate(pieces, axis=1)
        return (t[part].astype(jnp.float32) + summed.astype(jnp.float32)).astype(jnp.bfloat16)

    class Tail:
        def __init__(self, t):
            self.t = t
            self.gather_base = copies.take(4 * CHUNKS)
            self.pair_base, self.far_base, self.last_base = [copies.take(CHUNKS) for _ in range(3)]

        def attend(self):
            t, base = self.t, self.gather_base
            attended = attend(t)
            for j in range(CHUNKS):
                att_out[t, j] = attended(j).reshape(2, 8 * chunk, head_dim)
                for i, (h, target) in enumerate((
                    (half, mirror), (1 - half, {"ctx": 1 - half}), (1 - half, {"ctx": 3 - half}),
                )):
                    copy = copies.make(
                        base + 4 * j + i, att_out.at[t, j, h], att.at[t, j, me_ctx], target, base + 4 * j + me_ctx
                    )
                    copy.start()
                    sent.append(copy)
                att[t, j, me_ctx] = att_out[t, j, half]
                sent.extend([self.pair(j), self.far(j), self.last(j)])

        def pair(self, j):
            return copies.make(self.pair_base + j, pair_out.at[self.t, j], pair_in.at[self.t, j], core_peer)

        def far(self, j):
            return copies.make(self.far_base + j, far_out.at[self.t, j], far_in.at[self.t, j], far_peer)

        def last(self, j):
            return copies.make(
                self.last_base + j, fin_out.at[self.t, j, 1 - place], fin.at[self.t, j, column_half], mirror
            )

        def project(self, j):
            t = self.t
            for d in range(1, ctx):
                h = ctx_at(d)
                index = self.gather_base + 4 * j
                copies.make(index, att_out.at[t, j, 0], att.at[t, j, h], mirror, index + h).wait_recv()
            lhs = jnp.concatenate([att[t, j, h] for h in range(ctx)], axis=1)
            product = jnp.dot(lhs, wo[...], preferred_element_type=jnp.float32)
            product = product.reshape(2, 4, chunk, 2 * share)
            for n in range(2):
                pair_out[t, j, n] = product[:, 2 * n + 1].astype(jnp.bfloat16)
                keep[t, j, n] = product[:, 2 * n]
            self.pair(j).start()

        def sum_pair(self, j):
            t = self.t
            self.pair(j).wait_recv()
            far_out[t, j] = (keep[t, j, 1] + pair_in[t, j, 1].astype(jnp.float32)).astype(jnp.bfloat16)
            self.far(j).start()
            keep[t, j, 0] = keep[t, j, 0] + pair_in[t, j, 0].astype(jnp.float32)

        def sum_far(self, j):
            t = self.t
            self.far(j).wait_recv()
            fin_out[t, j] = (keep[t, j, 0] + far_in[t, j].astype(jnp.float32)).astype(jnp.bfloat16)

        def spread_sum(self, j):
            t = self.t
            self.last(j).start()
            fin[t, j, column_half] = fin_out[t, j, place]

        def sum_and_spread(self, j):
            self.sum_far(j)
            self.spread_sum(j)

        def sum_and_cross(self, j):
            self.sum_far(j)
            for crossing in crossings(j, column_half):
                crossing.start()

        def finish(self, j):
            t = self.t
            self.last(j).wait_recv()
            outbuf[t, pl.ds(j * chunk, chunk)] = finish_rows(xin.at[t], j, [fin[t, j, p] for p in range(2)])

        def run(self, order):
            stages = {
                "A": self.project, "B": self.sum_pair, "C": self.sum_and_spread, "X": self.sum_and_cross,
                "L": self.spread_sum, "D": self.finish,
            }
            for name in order:
                stages[name[0]](int(name[1]))

    cross_base = copies.take(2 * CHUNKS)

    def crossings(j, sender):
        across = {"section": 1 - me_section}
        return [
            copies.make(
                cross_base + 2 * j + i, fin_out.at[0, j, p], crossed.at[j, sender], target, cross_base + 2 * j + sender
            )
            for i, (p, target) in enumerate(((1 - place, mirror | across), (place, across)))
        ]

    def take_over(j):
        for p in range(2):
            crossings(j, p)[0].wait_recv()
        xin[1, pl.ds(j * chunk, chunk)] = finish_rows(before, j, [crossed[j, p] for p in range(2)])
        spread(1, j)

    def pass_on(j):
        far[1, j].wait_recv()
        relay[1, j].start()

    def begin_next(j, between=None):
        pieces = []
        if j < CHUNKS:
            near[1, j].wait_recv()
            pieces.append((0, j))
        if j > 0:
            relay[1, j - 1].wait_recv()
            pieces.append((1, j - 1))
        head_of_next(pieces, between)

    def swap_done():
        for swap in swaps:
            swap.wait_recv()
        wo[...] = wo_t[...].T

    def store(t):
        return pltpu.make_async_copy(outbuf.at[t], out.at[0, t], load_sems.at[steps + t])

    earlier, later = Tail(0), Tail(1)
    out_load.wait()
    earlier.attend()

    @pl.when(first_section)
    def _():
        for j in range(CHUNKS):
            near[1, j].wait_recv()
            relay[1, j].wait_recv()
        head_of_next_whole()
        send_next(0)
        swap_done()
        earlier.run(["A0", "B0", "A1", "B1", "A2", "X0", "B2", "X1", "X2"])
        for j in range(1, CHUNKS):
            send_next(j)
        earlier.run(["L0", "L1", "L2"])
        earlier.run(["D0", "D1", "D2"])
        store(0).start()

    @pl.when(last_section)
    def _():
        for swap in swaps[DIRECT:]:
            swap.start()
        ahead.wait_recv()
        take_over(0)
        begin_next(0)
        take_over(1)
        pass_on(0)
        take_over(2)
        begin_next(1, functools.partial(pass_on, 1))
        begin_next(2, functools.partial(pass_on, 2))
        begin_next(3)
        swap_done()
        earlier.run(["A0", "A1", "B0", "A2", "B1", "B2"])

    later.attend()

    @pl.when(last_section)
    def _():
        earlier.run(["C0", "C1"])

    later.run(["A0"])

    @pl.when(last_section)
    def _():
        earlier.run(["C2"])

    later.run(["B0", "A1", "B1", "A2", "C0", "B2", "C1", "C2"])

    @pl.when(last_section)
    def _():
        earlier.run(["D0", "D1", "D2"])
        store(0).start()

    later.run(["D0", "D1", "D2"])
    store(1).start()
    for t in range(steps):
        store(t).wait()
    for copy in sent:
        copy.wait_send()

    @pl.when(first_section)
    def _():
        for copy in detours + [ahead] + [copy for j in range(CHUNKS) for copy in crossings(j, column_half)]:
            copy.wait_send()

    @pl.when(last_section)
    def _():
        for copy in forwards + swaps[DIRECT:]:
            copy.wait_send()


def fused_device(patches, carried, norm_gain, q_gain, k_gain, q_weight, k_weight, v_weight, o_weight):
    steps, rows, width = patches.shape
    ctx = lax.axis_size("ctx")
    head_dim = q_gain.shape[1]
    columns = q_weight.shape[2]
    share = o_weight.shape[2]
    bf16, f32 = jnp.bfloat16, jnp.float32
    segment = 4 * rows
    chunk = rows // CHUNKS
    anywhere = pl.BlockSpec(memory_space=pl.ANY)
    vmem = pl.BlockSpec(memory_space=pltpu.VMEM)
    number = copies_needed(steps)
    flops = steps * 2 * segment * (3 * width * columns + ctx * columns * share + 2 * ctx * segment * columns)
    return pl.pallas_call(
        functools.partial(layer_kernel, steps, ctx),
        out_shape=jax.ShapeDtypeStruct((1, steps, rows, width), bf16),
        in_specs=[anywhere, anywhere, vmem, vmem, vmem, anywhere, anywhere, anywhere, anywhere],
        out_specs=anywhere,
        scratch_shapes=[
            pltpu.VMEM((steps, rows, width), bf16),
            pltpu.VMEM((rows, width), bf16),
            pltpu.VMEM((steps, 2, CHUNKS, 2, chunk, width), bf16),
            pltpu.VMEM((width, columns), bf16),
            pltpu.VMEM((width, columns), bf16),
            pltpu.VMEM((width, columns), bf16),
            pltpu.VMEM((share, columns), bf16),
            pltpu.VMEM((2 * share, columns), bf16),
            pltpu.VMEM((columns, 2 * share), bf16),
            pltpu.VMEM((2, ctx, 3, CHUNKS, 2 * chunk, head_dim), bf16),
            pltpu.VMEM((CHUNKS, ctx, 3, 4 * chunk, head_dim), bf16),
            pltpu.VMEM((steps, 3, CHUNKS, ctx, 4 * chunk, head_dim), bf16),
            pltpu.VMEM((steps, CHUNKS, ctx, 8 * chunk, head_dim), bf16),
            pltpu.VMEM((steps, CHUNKS, 2, 8 * chunk, head_dim), bf16),
            pltpu.VMEM((steps, CHUNKS, 2, 2, chunk, 2 * share), bf16),
            pltpu.VMEM((steps, CHUNKS, 2, 2, chunk, 2 * share), bf16),
            pltpu.VMEM((steps, CHUNKS, 2, 2, chunk, 2 * share), f32),
            pltpu.VMEM((steps, CHUNKS, 2, chunk, 2 * share), bf16),
            pltpu.VMEM((steps, CHUNKS, 2, chunk, 2 * share), bf16),
            pltpu.VMEM((steps, CHUNKS, 2, chunk, 2 * share), bf16),
            pltpu.VMEM((steps, CHUNKS, 2, chunk, 2 * share), bf16),
            pltpu.VMEM((CHUNKS, 2, chunk, 2 * share), bf16),
            pltpu.VMEM((steps, rows, width), bf16),
            pltpu.SemaphoreType.DMA((number,)),
            pltpu.SemaphoreType.DMA((number,)),
            pltpu.SemaphoreType.DMA((2 * steps + 1 + 3 * (columns // head_dim),)),
        ],
        compiler_params=pltpu.CompilerParams(
            collective_id=0, has_side_effects=True, vmem_limit_bytes=56 * 2**20
        ),
        cost_estimate=pl.CostEstimate(flops=flops, bytes_accessed=12 * 2**20, transcendentals=0),
    )(patches, carried, norm_gain, q_gain, k_gain, q_weight, k_weight, v_weight, jnp.swapaxes(o_weight, 1, 2))


def solution(mesh):
    in_specs = (
        P(None, ("ctx", "mp"), None),
        P(("ctx", "mp"), None),
        P("section", None),
        P("section", None),
        P("section", None),
        P("section", None, "mp"),
        P("section", None, "mp"),
        P("section", None, "mp"),
        P("section", "mp", "ctx"),
    )
    out_specs = P("section", None, ("ctx", "mp"), None)

    def program(*arrays):
        ctx, mp, sections = mesh.shape["ctx"], mesh.shape["mp"], mesh.shape["section"]
        heads = arrays[5].shape[2] // arrays[3].shape[1]
        rows = arrays[1].shape[0] // (ctx * mp)
        fits = mp == 4 and sections == 2 and ctx * mp == heads and ctx == 4 and rows == 16 * CHUNKS
        fits = fits and arrays[0].shape[0] == 2 and arrays[8].shape[2] % (16 * SWAPS * ctx) == 0
        body = fused_device if fits else per_device
        return jax.shard_map(body, mesh=mesh, in_specs=in_specs, out_specs=out_specs, check_vma=False)(*arrays)

    return program
```

```python
import functools
import math

import jax
import jax.numpy as jnp
from jax import lax
from jax.experimental import pallas as pl
from jax.experimental.pallas import tpu as pltpu
from jax.sharding import PartitionSpec as P

epsilon = 1e-06


def rms_scaled(values, gain):
    return values * lax.rsqrt(jnp.mean(values * values, axis=-1, keepdims=True) + epsilon) * gain


def shifted(value, axis, steps):
    count = lax.axis_size(axis)
    leading, last = (max(0, -steps), min(count, count - steps))
    return lax.ppermute(value, axis, [(source, source + steps) for source in range(leading, last)])


def per_device(patches, carried, norm_gain, q_gain, k_gain, q_weight, k_weight, v_weight, o_weight):
    micro_count = patches.shape[0]
    head_dim = q_gain.shape[1]
    head_count = q_weight.shape[2] // head_dim
    columns = head_count * head_dim
    score_scale = 1.0 / math.sqrt(head_dim)
    section_index = lax.axis_index("section")
    incoming = carried
    results = []
    out_weight = lax.all_gather(o_weight[0], "ctx", axis=1, tiled=True)
    for micro_step in range(micro_count):
        layer_input = jnp.where(section_index == 0, patches[micro_step], incoming)
        residual = layer_input.astype(jnp.float32)
        normed = rms_scaled(residual, norm_gain[0]).astype(jnp.bfloat16)
        segment = lax.all_gather(normed, "mp", axis=0, tiled=True)
        rows = segment.shape[0]
        raw_query = jnp.dot(segment, q_weight[0], preferred_element_type=jnp.float32)
        raw_key = jnp.dot(segment, k_weight[0], preferred_element_type=jnp.float32)
        raw_value = jnp.dot(segment, v_weight[0], preferred_element_type=jnp.float32)
        queries = rms_scaled(raw_query.reshape(rows, head_count, head_dim), q_gain[0])
        keys = rms_scaled(raw_key.reshape(rows, head_count, head_dim), k_gain[0])
        keys = keys.astype(jnp.bfloat16).reshape(rows, columns)
        key_block = lax.all_gather(keys, "ctx", axis=0, tiled=True)
        value_block = lax.all_gather(raw_value.astype(jnp.bfloat16), "ctx", axis=0, tiled=True)
        count = key_block.shape[0]
        scores = score_scale * jnp.einsum(
            "qhd,khd->qhk",
            queries.astype(jnp.bfloat16),
            key_block.reshape(count, head_count, head_dim),
            preferred_element_type=jnp.float32,
        )
        probs = jnp.exp(scores)
        totals = jnp.sum(probs, axis=2)
        weighted = jnp.einsum(
            "qhk,khd->qhd",
            probs.astype(jnp.bfloat16),
            value_block.reshape(count, head_count, head_dim),
            preferred_element_type=jnp.float32,
        )
        attended = (weighted / totals[:, :, None]).reshape(rows, columns).astype(jnp.bfloat16)
        partial_value = jnp.dot(attended, out_weight, preferred_element_type=jnp.float32)
        summed = lax.psum_scatter(partial_value, "mp", scatter_dimension=0, tiled=True)
        layer_out = (residual + summed).astype(jnp.bfloat16)
        results.append(layer_out)
        if micro_step + 1 < micro_count:
            incoming = shifted(layer_out, "section", 1)
    return jnp.stack(results)[None]


CHUNKS = 3
SWAPS = 10
DIRECT = 4


class Copies:
    def __init__(self, send_sems, recv_sems):
        self.send_sems, self.recv_sems, self.used = send_sems, recv_sems, 0

    def take(self, count):
        first = self.used
        self.used += count
        return first

    def make(self, index, source, target, device, recv=None):
        return pltpu.make_async_remote_copy(
            src_ref=source,
            dst_ref=target,
            send_sem=self.send_sems.at[index],
            recv_sem=self.recv_sems.at[index if recv is None else recv],
            device_id=device,
            device_id_type=pl.DeviceIdType.MESH,
        )


def copies_needed(steps):
    return 2 * SWAPS + 1 + 3 * CHUNKS * steps + 4 * 2 + 4 * CHUNKS * (steps - 1) + steps * CHUNKS * (4 + 3) + 2 * CHUNKS


def layer_kernel(
    steps, ctx,
    patches, carried, norm_gain, q_gain, k_gain, q_weight, k_weight, v_weight, o_weight,
    out,
    xin, before, xn, wq, wk, wv, stage, wo_t, wo, heads_first, heads_next, qkv,
    att, att_out, pair_out, pair_in, keep, far_out, far_in, fin_out, fin, crossed, outbuf,
    send_sems, recv_sems, load_sems,
):
    me_ctx = lax.axis_index("ctx")
    me_section = lax.axis_index("section")
    me_mp = lax.axis_index("mp")
    core_peer = {"mp": me_mp + 1 - 2 * lax.rem(me_mp, 2)}
    far_peer = {"mp": lax.rem(me_mp + 2, 4)}
    section_peer = {"section": 1 - me_section}
    swap_peer = {"ctx": me_ctx + 1 - 2 * lax.rem(me_ctx, 2)}
    half = lax.rem(me_ctx, 2)
    place = me_ctx // 2
    slot = 2 * half + place
    column_half = me_ctx // 2
    mirror = {"ctx": lax.rem(me_ctx + 2, ctx)}

    def ctx_at(offset):
        return lax.rem(me_ctx + offset + ctx, ctx)

    head_dim = q_gain.shape[1]
    head_count = q_weight.shape[2] // head_dim
    width = xin.shape[2]
    rows = xin.shape[1]
    chunk = rows // CHUNKS
    share = o_weight.shape[1]
    scale = math.log2(math.e) / math.sqrt(head_dim)
    first_section = me_section == 0
    last_section = me_section == 1

    patch_loads = [pltpu.make_async_copy(patches.at[t], xin.at[t], load_sems.at[t]) for t in range(steps)]
    carried_load = pltpu.make_async_copy(carried, xin.at[0], load_sems.at[0])

    @pl.when(first_section)
    def _():
        for load in patch_loads:
            load.start()

    @pl.when(last_section)
    def _():
        carried_load.start()

    head_order = [h for n in range(head_count // 2) for h in (n, head_count - 1 - n)]
    weight_loads = []
    for position, h in enumerate(head_order):
        for n, (source, target) in enumerate(((q_weight, wq), (k_weight, wk), (v_weight, wv))):
            weight_loads.append(
                pltpu.make_async_copy(
                    source.at[0, :, pl.ds(h * head_dim, head_dim)],
                    target.at[:, pl.ds(position * head_dim, head_dim)],
                    load_sems.at[2 * steps + 1 + position * 3 + n],
                )
            )
    own_columns = pl.ds(pl.multiple_of(lax.rem(me_ctx, 2) * share, 16), share)
    out_load = pltpu.make_async_copy(o_weight.at[0], wo_t.at[own_columns], load_sems.at[2 * steps])
    for load in weight_loads + [out_load]:
        load.start()

    barrier = pltpu.get_barrier_semaphore()
    peers = [core_peer, far_peer, section_peer] + [{"ctx": ctx_at(d)} for d in range(1, ctx)]
    peers += [{"ctx": ctx_at(d), "section": 1 - me_section} for d in range(1, ctx)]
    for peer in peers:
        pl.semaphore_signal(barrier, inc=1, device_id=peer, device_id_type=pl.DeviceIdType.MESH)
    pl.semaphore_wait(barrier, len(peers))

    copies = Copies(send_sems, recv_sems)
    sent = []

    base, detour_base = copies.take(SWAPS), copies.take(SWAPS)
    swaps, detours, forwards = [], [], []
    part = share // SWAPS
    for i in range(SWAPS):
        source = o_weight.at[0, pl.ds(i * part, part)]
        target = wo_t.at[pl.ds(pl.multiple_of(lax.rem(me_ctx, 2) * share + i * part, 16), part)]
        swaps.append(copies.make(base + i, source, target, swap_peer))
        if i >= DIRECT:
            between = stage.at[pl.ds(i * part, part)]
            detours.append(copies.make(detour_base + i, source, between, section_peer))
            forwards.append(
                copies.make(detour_base + i, between, target, swap_peer | {"section": 1 - me_section}, base + i)
            )
    sent += swaps[:DIRECT]
    ahead = copies.make(copies.take(1), patches.at[0], before, section_peer)

    @pl.when(first_section)
    def _():
        for detour in detours:
            detour.start()
        ahead.start()

    near, far, relay = {}, {}, {}
    for t in range(steps):
        base = copies.take(3 * CHUNKS)
        for j in range(CHUNKS):
            own = xn.at[t, 0, j, 0]
            far[t, j] = copies.make(base + j, own, xn.at[t, 1, j, 0], far_peer)
            near[t, j] = copies.make(base + CHUNKS + j, own, xn.at[t, 0, j, 1], core_peer)
            relay[t, j] = copies.make(base + 2 * CHUNKS + j, xn.at[t, 1, j, 0], xn.at[t, 1, j, 1], core_peer)
    for group in (near, far, relay):
        sent += list(group.values())

    def spread(t, j):
        values = xin[t, pl.ds(j * chunk, chunk)].astype(jnp.float32)
        xn[t, 0, j, 0] = rms_scaled(values, norm_gain[...]).astype(jnp.bfloat16)
        far[t, j].start()
        near[t, j].start()

    def project_heads(lhs, keep_part, send_part, loads=None, between=None):
        for first in range(0, head_count, 2):
            if first > 0 and between is not None:
                between()
            if loads is not None:
                for load in loads[3 * first:3 * (first + 2)]:
                    load.wait()
            lanes = pl.ds(first * head_dim, 2 * head_dim)
            raw = [jnp.dot(lhs, w[:, lanes], preferred_element_type=jnp.float32) for w in (wq, wk, wv)]
            for side in range(2):
                h = head_order[first + side]
                own = slice(side * head_dim, (side + 1) * head_dim)
                parts = [
                    rms_scaled(raw[0][:, own], q_gain[...]).astype(jnp.bfloat16),
                    rms_scaled(raw[1][:, own], k_gain[...]).astype(jnp.bfloat16),
                    raw[2][:, own].astype(jnp.bfloat16),
                ]

                @pl.when(me_ctx == h)
                def _():
                    for n in range(3):
                        keep_part(n, parts[n])

                @pl.when(me_ctx != h)
                def _():
                    for n in range(3):
                        send_part(h, n, parts[n])
                    send_part(h, None, None)

    two = 2 * chunk
    first_bases = [copies.take(ctx) for _ in range(2)]
    next_bases = [copies.take(ctx) for _ in range(CHUNKS)]

    def first_slab(g, h):
        return heads_first.at[g, h]

    def first_target(g):
        return qkv.at[0, :, :, slot, pl.ds(g * two, two)]

    def next_slab(j, h):
        return heads_next.at[j, h]

    def next_target(j):
        return qkv.at[1, :, j, slot]

    def head_of_first(g, loads=None):
        def keep_part(n, value):
            qkv[0, n, :, slot, pl.ds(g * two, two)] = value.reshape(CHUNKS, two, head_dim)

        def send_part(h, n, value):
            if n is None:
                d = lax.rem(h - me_ctx + ctx, ctx)
                copies.make(first_bases[g] + d, first_slab(g, h), first_target(g), {"ctx": h}).start()
            else:
                heads_first[g, h, n] = value.reshape(CHUNKS, two, head_dim)

        project_heads(xn[0, g].reshape(CHUNKS * two, width), keep_part, send_part, loads)

    def head_of_next_whole():
        def keep_part(n, value):
            for g in range(2):
                piece = value[g * CHUNKS * two:(g + 1) * CHUNKS * two].reshape(CHUNKS, two, head_dim)
                qkv[1, n, :, slot, pl.ds(g * two, two)] = piece

        def send_part(h, n, value):
            if n is not None:
                for g in range(2):
                    piece = value[g * CHUNKS * two:(g + 1) * CHUNKS * two].reshape(CHUNKS, two, head_dim)
                    heads_next[:, h, n, pl.ds(g * two, two)] = piece

        project_heads(xn[1].reshape(2 * CHUNKS * two, width), keep_part, send_part)

    def send_next(j):
        for d in (2, 1, ctx - 1):
            next_arrival(j, d).start()

    def next_arrival(j, d):
        return copies.make(next_bases[j] + d, next_slab(j, ctx_at(d)), next_target(j), {"ctx": ctx_at(d)})

    def head_of_next(pieces, between=None):
        def keep_part(n, value):
            for i, (g, j) in enumerate(pieces):
                qkv[1, n, j, slot, pl.ds(g * two, two)] = value[i * two:(i + 1) * two]

        def send_part(h, n, value):
            for i, (g, j) in enumerate(pieces):
                if n is None:
                    d = lax.rem(h - me_ctx + ctx, ctx)
                    part = pl.ds(g * two, two)
                    copies.make(
                        next_bases[j] + d, heads_next.at[j, h, :, part], qkv.at[1, :, j, slot, part], {"ctx": h}
                    ).start()
                else:
                    heads_next[j, h, n, pl.ds(g * two, two)] = value[i * two:(i + 1) * two]

        lhs = jnp.concatenate([xn[1, g, j].reshape(two, width) for g, j in pieces], axis=0)
        project_heads(lhs, keep_part, send_part, between=between)

    arrivals = {0: [], 1: []}
    for d in range(1, ctx):
        for g in range(2):
            arrivals[0].append(
                copies.make(first_bases[g] + d, first_slab(g, ctx_at(d)), first_target(g), {"ctx": ctx_at(d)})
            )
        for j in range(CHUNKS):
            arrivals[1].append(next_arrival(j, d))
    sent += arrivals[0] + arrivals[1]

    for swap in swaps[:2]:
        swap.start()
    carried_load.wait()
    for j in range(CHUNKS):
        spread(0, j)

    @pl.when(first_section)
    def _():
        patch_loads[1].wait()
        for j in range(CHUNKS):
            spread(1, j)

    for j in range(CHUNKS):
        near[0, j].wait_recv()
    head_of_first(0, weight_loads)
    for swap in swaps[2:DIRECT]:
        swap.start()

    @pl.when(last_section)
    def _():
        for detour, forward in zip(detours, forwards):
            detour.wait_recv()
            forward.start()

    for j in range(CHUNKS):
        far[0, j].wait_recv()
        relay[0, j].start()
    for j in range(CHUNKS):
        relay[0, j].wait_recv()
    head_of_first(1)

    @pl.when(first_section)
    def _():
        for j in range(CHUNKS):
            far[1, j].wait_recv()
            relay[1, j].start()

    def attend(t):
        for arrival in arrivals[t]:
            arrival.wait_recv()
        keys = qkv[t, 1].reshape(CHUNKS * 4 * ctx * chunk, head_dim)
        vals = qkv[t, 2].reshape(CHUNKS * 4 * ctx * chunk, head_dim)

        def attended(j):
            scores = lax.dot_general(
                qkv[t, 0, j].reshape(4 * ctx * chunk, head_dim), keys, (((1,), (1,)), ((), ())),
                preferred_element_type=jnp.float32,
            )
            probs = jnp.exp2(scores * scale)
            totals = jnp.sum(probs, axis=1, keepdims=True)
            weighted = jnp.dot(probs.astype(jnp.bfloat16), vals, preferred_element_type=jnp.float32)
            return (weighted / totals).astype(jnp.bfloat16)

        return attended

    def finish_rows(t, j, pieces):
        part = pl.ds(j * chunk, chunk)
        summed = jnp.concatenate(pieces, axis=1)
        return (t[part].astype(jnp.float32) + summed.astype(jnp.float32)).astype(jnp.bfloat16)

    class Tail:
        def __init__(self, t):
            self.t = t
            self.gather_base = copies.take(4 * CHUNKS)
            self.pair_base, self.far_base, self.last_base = [copies.take(CHUNKS) for _ in range(3)]

        def attend(self):
            t, base = self.t, self.gather_base
            attended = attend(t)
            for j in range(CHUNKS):
                att_out[t, j] = attended(j).reshape(2, 8 * chunk, head_dim)
                for i, (h, target) in enumerate((
                    (half, mirror), (1 - half, {"ctx": 1 - half}), (1 - half, {"ctx": 3 - half}),
                )):
                    copy = copies.make(
                        base + 4 * j + i, att_out.at[t, j, h], att.at[t, j, me_ctx], target, base + 4 * j + me_ctx
                    )
                    copy.start()
                    sent.append(copy)
                att[t, j, me_ctx] = att_out[t, j, half]
                sent.extend([self.pair(j), self.far(j), self.last(j)])

        def pair(self, j):
            return copies.make(self.pair_base + j, pair_out.at[self.t, j], pair_in.at[self.t, j], core_peer)

        def far(self, j):
            return copies.make(self.far_base + j, far_out.at[self.t, j], far_in.at[self.t, j], far_peer)

        def last(self, j):
            return copies.make(
                self.last_base + j, fin_out.at[self.t, j, 1 - place], fin.at[self.t, j, column_half], mirror
            )

        def project(self, j):
            t = self.t
            for d in range(1, ctx):
                h = ctx_at(d)
                index = self.gather_base + 4 * j
                copies.make(index, att_out.at[t, j, 0], att.at[t, j, h], mirror, index + h).wait_recv()
            lhs = jnp.concatenate([att[t, j, h] for h in range(ctx)], axis=1)
            product = jnp.dot(lhs, wo[...], preferred_element_type=jnp.float32)
            product = product.reshape(2, 4, chunk, 2 * share)
            for n in range(2):
                pair_out[t, j, n] = product[:, 2 * n + 1].astype(jnp.bfloat16)
                keep[t, j, n] = product[:, 2 * n]
            self.pair(j).start()

        def sum_pair(self, j):
            t = self.t
            self.pair(j).wait_recv()
            far_out[t, j] = (keep[t, j, 1] + pair_in[t, j, 1].astype(jnp.float32)).astype(jnp.bfloat16)
            self.far(j).start()
            keep[t, j, 0] = keep[t, j, 0] + pair_in[t, j, 0].astype(jnp.float32)

        def sum_far(self, j):
            t = self.t
            self.far(j).wait_recv()
            fin_out[t, j] = (keep[t, j, 0] + far_in[t, j].astype(jnp.float32)).astype(jnp.bfloat16)

        def spread_sum(self, j):
            t = self.t
            self.last(j).start()
            fin[t, j, column_half] = fin_out[t, j, place]

        def sum_and_spread(self, j):
            self.sum_far(j)
            self.spread_sum(j)

        def sum_and_cross(self, j):
            self.sum_far(j)
            for crossing in crossings(j, column_half):
                crossing.start()

        def finish(self, j):
            t = self.t
            self.last(j).wait_recv()
            outbuf[t, pl.ds(j * chunk, chunk)] = finish_rows(xin.at[t], j, [fin[t, j, p] for p in range(2)])

        def run(self, order):
            stages = {
                "A": self.project, "B": self.sum_pair, "C": self.sum_and_spread, "X": self.sum_and_cross,
                "L": self.spread_sum, "D": self.finish,
            }
            for name in order:
                stages[name[0]](int(name[1]))

    cross_base = copies.take(2 * CHUNKS)

    def crossings(j, sender):
        across = {"section": 1 - me_section}
        return [
            copies.make(
                cross_base + 2 * j + i, fin_out.at[0, j, p], crossed.at[j, sender], target, cross_base + 2 * j + sender
            )
            for i, (p, target) in enumerate(((1 - place, mirror | across), (place, across)))
        ]

    def take_over(j):
        for p in range(2):
            crossings(j, p)[0].wait_recv()
        xin[1, pl.ds(j * chunk, chunk)] = finish_rows(before, j, [crossed[j, p] for p in range(2)])
        spread(1, j)

    def pass_on(j):
        far[1, j].wait_recv()
        relay[1, j].start()

    def begin_next(j, between=None):
        pieces = []
        if j < CHUNKS:
            near[1, j].wait_recv()
            pieces.append((0, j))
        if j > 0:
            relay[1, j - 1].wait_recv()
            pieces.append((1, j - 1))
        head_of_next(pieces, between)

    def swap_done():
        for swap in swaps:
            swap.wait_recv()
        wo[...] = wo_t[...].T

    def store(t):
        return pltpu.make_async_copy(outbuf.at[t], out.at[0, t], load_sems.at[steps + t])

    earlier, later = Tail(0), Tail(1)
    out_load.wait()
    earlier.attend()

    @pl.when(first_section)
    def _():
        for j in range(CHUNKS):
            near[1, j].wait_recv()
            relay[1, j].wait_recv()
        head_of_next_whole()
        swap_done()
        earlier.run(["A0", "B0", "A1", "B1", "A2", "X0", "B2", "X1", "X2"])
        for j in range(CHUNKS):
            send_next(j)
        earlier.run(["L0", "L1", "L2"])
        earlier.run(["D0", "D1", "D2"])
        store(0).start()

    @pl.when(last_section)
    def _():
        for swap in swaps[DIRECT:]:
            swap.start()
        ahead.wait_recv()
        take_over(0)
        begin_next(0)
        take_over(1)
        pass_on(0)
        take_over(2)
        begin_next(1, functools.partial(pass_on, 1))
        begin_next(2, functools.partial(pass_on, 2))
        begin_next(3)
        swap_done()
        earlier.run(["A0", "A1", "B0", "A2", "B1", "B2"])

    later.attend()

    @pl.when(last_section)
    def _():
        earlier.run(["C0", "C1"])

    later.run(["A0"])

    @pl.when(last_section)
    def _():
        earlier.run(["C2"])

    later.run(["B0", "A1", "B1", "A2", "C0", "B2", "C1", "C2"])

    @pl.when(last_section)
    def _():
        earlier.run(["D0", "D1", "D2"])
        store(0).start()

    later.run(["D0", "D1", "D2"])
    store(1).start()
    for t in range(steps):
        store(t).wait()
    for copy in sent:
        copy.wait_send()

    @pl.when(first_section)
    def _():
        for copy in detours + [ahead] + [copy for j in range(CHUNKS) for copy in crossings(j, column_half)]:
            copy.wait_send()

    @pl.when(last_section)
    def _():
        for copy in forwards + swaps[DIRECT:]:
            copy.wait_send()


def fused_device(patches, carried, norm_gain, q_gain, k_gain, q_weight, k_weight, v_weight, o_weight):
    steps, rows, width = patches.shape
    ctx = lax.axis_size("ctx")
    head_dim = q_gain.shape[1]
    columns = q_weight.shape[2]
    share = o_weight.shape[2]
    bf16, f32 = jnp.bfloat16, jnp.float32
    segment = 4 * rows
    chunk = rows // CHUNKS
    anywhere = pl.BlockSpec(memory_space=pl.ANY)
    vmem = pl.BlockSpec(memory_space=pltpu.VMEM)
    number = copies_needed(steps)
    flops = steps * 2 * segment * (3 * width * columns + ctx * columns * share + 2 * ctx * segment * columns)
    return pl.pallas_call(
        functools.partial(layer_kernel, steps, ctx),
        out_shape=jax.ShapeDtypeStruct((1, steps, rows, width), bf16),
        in_specs=[anywhere, anywhere, vmem, vmem, vmem, anywhere, anywhere, anywhere, anywhere],
        out_specs=anywhere,
        scratch_shapes=[
            pltpu.VMEM((steps, rows, width), bf16),
            pltpu.VMEM((rows, width), bf16),
            pltpu.VMEM((steps, 2, CHUNKS, 2, chunk, width), bf16),
            pltpu.VMEM((width, columns), bf16),
            pltpu.VMEM((width, columns), bf16),
            pltpu.VMEM((width, columns), bf16),
            pltpu.VMEM((share, columns), bf16),
            pltpu.VMEM((2 * share, columns), bf16),
            pltpu.VMEM((columns, 2 * share), bf16),
            pltpu.VMEM((2, ctx, 3, CHUNKS, 2 * chunk, head_dim), bf16),
            pltpu.VMEM((CHUNKS, ctx, 3, 4 * chunk, head_dim), bf16),
            pltpu.VMEM((steps, 3, CHUNKS, ctx, 4 * chunk, head_dim), bf16),
            pltpu.VMEM((steps, CHUNKS, ctx, 8 * chunk, head_dim), bf16),
            pltpu.VMEM((steps, CHUNKS, 2, 8 * chunk, head_dim), bf16),
            pltpu.VMEM((steps, CHUNKS, 2, 2, chunk, 2 * share), bf16),
            pltpu.VMEM((steps, CHUNKS, 2, 2, chunk, 2 * share), bf16),
            pltpu.VMEM((steps, CHUNKS, 2, 2, chunk, 2 * share), f32),
            pltpu.VMEM((steps, CHUNKS, 2, chunk, 2 * share), bf16),
            pltpu.VMEM((steps, CHUNKS, 2, chunk, 2 * share), bf16),
            pltpu.VMEM((steps, CHUNKS, 2, chunk, 2 * share), bf16),
            pltpu.VMEM((steps, CHUNKS, 2, chunk, 2 * share), bf16),
            pltpu.VMEM((CHUNKS, 2, chunk, 2 * share), bf16),
            pltpu.VMEM((steps, rows, width), bf16),
            pltpu.SemaphoreType.DMA((number,)),
            pltpu.SemaphoreType.DMA((number,)),
            pltpu.SemaphoreType.DMA((2 * steps + 1 + 3 * (columns // head_dim),)),
        ],
        compiler_params=pltpu.CompilerParams(
            collective_id=0, has_side_effects=True, vmem_limit_bytes=56 * 2**20
        ),
        cost_estimate=pl.CostEstimate(flops=flops, bytes_accessed=12 * 2**20, transcendentals=0),
    )(patches, carried, norm_gain, q_gain, k_gain, q_weight, k_weight, v_weight, jnp.swapaxes(o_weight, 1, 2))


def solution(mesh):
    in_specs = (
        P(None, ("ctx", "mp"), None),
        P(("ctx", "mp"), None),
        P("section", None),
        P("section", None),
        P("section", None),
        P("section", None, "mp"),
        P("section", None, "mp"),
        P("section", None, "mp"),
        P("section", "mp", "ctx"),
    )
    out_specs = P("section", None, ("ctx", "mp"), None)

    def program(*arrays):
        ctx, mp, sections = mesh.shape["ctx"], mesh.shape["mp"], mesh.shape["section"]
        heads = arrays[5].shape[2] // arrays[3].shape[1]
        rows = arrays[1].shape[0] // (ctx * mp)
        fits = mp == 4 and sections == 2 and ctx * mp == heads and ctx == 4 and rows == 16 * CHUNKS
        fits = fits and arrays[0].shape[0] == 2 and arrays[8].shape[2] % (16 * SWAPS * ctx) == 0
        body = fused_device if fits else per_device
        return jax.shard_map(body, mesh=mesh, in_specs=in_specs, out_specs=out_specs, check_vma=False)(*arrays)

    return program
```
